256 devices in a mesh: section: 4 (over y), seq: 16 (over z_lo, x, core), head: 4 (over z_hi).
Axes of the slice: x: 4, y: 4, z: 8 (z_hi: 4, z_lo: 2; z = z_hi * 2 + z_lo), core: 2. Of those that a mesh axis runs over, the one named last changes fastest.
Arguments:
- encoder_states: bfloat16 [4, 2048, 4096], P(None, 'seq'), may hold values from -6 to 6
- w_kv: bfloat16 [4, 4096, 4096], P(None, None, ('section', 'head')), may hold values from -0.125 to 0.125
- queries: bfloat16 [4, 4, 256, 4, 512], P('section', None, None, None, 'head'), may hold values from -102 to 102
- cotangent: bfloat16 [4, 4, 256, 4, 512], P('section', None, None, None, 'head'), may hold values from -6 to 6
- src_len: int32 [4], replicated, may hold values from 512 to 2048, as said below
- tgt_len: int32 [4], replicated, may hold values from 64 to 256, as said below
Outputs:
- attn_out: bfloat16 [4, 4, 256, 4, 512], P('section', None, 'seq', None, 'head')
- query_grads: bfloat16 [4, 4, 256, 4, 512], P('section', None, 'seq', None, 'head')
- source_grads: bfloat16 [4, 2048, 4096], P(None, 'seq', ('section', 'head'))
The draws below stay inside these ranges and needn't reach their ends.
Inputs may be any that keep to these rules, and one draw needn't show every extreme that they name: `src_len`: at least one sample has all 2048 source tokens. `tgt_len`: at least one sample has all 256 target tokens.
All inputs are finite; a program needn't handle non-finite values.
Results may differ from the reference program's by a relative error of at most 0.014.
The reference program's roundings to bfloat16 on the way (of `key_value`, `probability_low`, `grad_out`, `grad_scores` and `grad_pairs`) count: a program that leaves them out, or rounds other values in their place, can miss the bound.
Values may be sent and summed in bfloat16 or wider, within the bound.
No kernel may reach another device: no remote copies, remote signals or barrier semaphores. Data moves between devices by JAX's collectives and lax.ppermute only.
A program may use at most 128 MiB of HBM per device.

```python
import jax
import jax.numpy as jnp
from jax import lax

D = 4096
HD = 128
BATCH = 4
SRC = 2048
TQ = 256
LAYERS = 4
GROUPS = 4
HEAD_COLS = 512
HEADS = 16


def target_lengths(key):
    lengths_drawn = jax.random.randint(key, (BATCH,), TQ // 4, TQ + 1)
    full_row = jax.random.randint(jax.random.fold_in(key, 13), (), 0, BATCH)
    return jnp.where(jnp.arange(BATCH) == full_row, TQ, lengths_drawn).astype(jnp.int32)


def draw_queries(key, part):
    shape = (LAYERS, BATCH, TQ, GROUPS, HEAD_COLS)
    base_key = jax.random.fold_in(key, 3)
    return jnp.clip(jax.random.normal(base_key, shape, jnp.float32), -6.0, 6.0).astype(jnp.bfloat16)


def draw_src_len(key, part):
    lengths_drawn = jax.random.randint(key, (BATCH,), SRC // 4, SRC + 1)
    full_row = jax.random.randint(jax.random.fold_in(key, 11), (), 0, BATCH)
    return jnp.where(jnp.arange(BATCH) == full_row, SRC, lengths_drawn).astype(jnp.int32)


def draw_tgt_len(key, part):
    return target_lengths(key)


def with_spikes(result, stream_key, source, target, parts, factor):
    def block_of(dim):
        return (jnp.arange(result.shape[dim]) // (result.shape[dim] // parts)).reshape((-1,) + (1,) * (result.ndim - 1 - dim))

    first = jax.random.permutation(stream_key, parts)[block_of(target)]
    far = (block_of(target) + parts // 2) % parts
    return jnp.where((block_of(source) == first) | (block_of(source) == far), factor * result, result)


def shard_levels(key, extent, cuts, least, high):
    level = 1.0
    for axis_at, shards_of in cuts:
        steps = jax.random.uniform(jax.random.fold_in(jax.random.fold_in(key, 6), axis_at), (shards_of,), jnp.float32, least / len(cuts), high / len(cuts))
        level = level * jnp.repeat(jnp.exp(steps), extent[axis_at] // shards_of).reshape((-1,) + (1,) * (len(extent) - 1 - axis_at))
    return level


def centred(stream_key, dims, scale, reach, pieces=(), kind=jnp.bfloat16):
    loudness = shard_levels(stream_key, dims, pieces, -0.22, 0.18) if pieces else 1.0
    values = jax.random.normal(stream_key, dims, jnp.float32) * scale * loudness
    return jnp.minimum(jnp.maximum(values, -reach), reach).astype(kind)


def gaussian_with(stream_key, extent, spread, limit, pieces, heavy, kind=jnp.bfloat16):
    drawn = spread * jax.random.normal(stream_key, extent, jnp.float32)
    if pieces:
        drawn = drawn * shard_levels(stream_key, extent, pieces, -0.22, 0.18)
    return jnp.clip(with_spikes(drawn, jax.random.fold_in(stream_key, 3), *heavy), -limit, limit).astype(kind)


def setup_inputs(seed: int = 0) -> dict:
    key_of = jax.random.split(jax.random.key(seed), 7)
    encoder_states = centred(key_of[0], (BATCH, SRC, D), 1.0, 6.0, ((1, 16),))
    w_kv = gaussian_with(key_of[1], (LAYERS, D, HEADS * 2 * HD), D ** -0.5, 0.125, ((2, 16),), (2, 1, 16, 2.0))
    queries = draw_queries(jax.random.fold_in(key_of[6], 71), 0)
    cotangent = centred(key_of[3], (LAYERS, BATCH, TQ, GROUPS, HEAD_COLS), 1.0, 6.0, ((0, 4), (4, 4)))
    src_len = draw_src_len(jax.random.fold_in(key_of[6], 71), 0)
    tgt_len = draw_tgt_len(jax.random.fold_in(key_of[6], 71), 0)
    return {"encoder_states": encoder_states, "w_kv": w_kv, "queries": queries, "cotangent": cotangent, "src_len": src_len, "tgt_len": tgt_len}


masked_score = -1e30


def round_low(value):
    low = value.astype(jnp.bfloat16)
    low = lax.optimization_barrier(low)
    return low.astype(jnp.float32)


def layer_grads(encoder_states, w_layer, query_layer, cot_layer, src_len, tgt_len):
    score_scale = HD ** -0.5
    key_value = jnp.einsum("bsd,dc->bsc", encoder_states.astype(jnp.float32), w_layer.astype(jnp.float32))
    key_value = round_low(key_value).reshape(BATCH, SRC, HEADS, 2, HD)
    key_rows = key_value[:, :, :, 0, :]
    value_rows = key_value[:, :, :, 1, :]
    query_rows = query_layer.astype(jnp.float32).reshape(BATCH, TQ, HEADS, HD)
    scores = jnp.einsum("bthd,bshd->bhts", query_rows, key_rows) * score_scale
    key_live = jnp.arange(SRC, dtype=jnp.int32)[None, :] < src_len[:, None]
    scores = jnp.where(key_live[:, None, None, :], scores, masked_score)
    row_top = jnp.max(scores, axis=-1, keepdims=True)
    exponent = jnp.exp(scores - row_top)
    row_total = jnp.sum(exponent, axis=-1, keepdims=True)
    probability = exponent / row_total
    probability_low = round_low(probability)
    attended = jnp.einsum("bhts,bshd->bthd", probability_low, value_rows)
    out_layer = attended.astype(jnp.bfloat16).reshape(BATCH, TQ, GROUPS, HEAD_COLS)
    query_live = jnp.arange(TQ, dtype=jnp.int32)[None, :] < tgt_len[:, None]
    grad_out = jnp.where(query_live[:, :, None, None], cot_layer.astype(jnp.float32).reshape(BATCH, TQ, HEADS, HD), jnp.float32(0.0))
    row_delta = jnp.transpose(jnp.sum(grad_out * attended, axis=-1), (0, 2, 1))
    grad_probs = jnp.einsum("bthd,bshd->bhts", grad_out, value_rows)
    grad_scores = round_low(probability * (grad_probs - row_delta[..., None]))
    grad_query = (score_scale * jnp.einsum("bhts,bshd->bthd", grad_scores, key_rows)).astype(jnp.bfloat16)
    grad_keys = score_scale * jnp.einsum("bhts,bthd->bshd", grad_scores, query_rows)
    grad_values = jnp.einsum("bhts,bthd->bshd", probability_low, grad_out)
    grad_pairs = round_low(jnp.stack([grad_keys, grad_values], axis=3)).reshape(BATCH, SRC, HEADS * 2 * HD)
    source_part = jnp.einsum("bsc,dc->bsd", grad_pairs, w_layer.astype(jnp.float32))
    return out_layer, grad_query.reshape(BATCH, TQ, GROUPS, HEAD_COLS), source_part


def reference(encoder_states, w_kv, queries, cotangent, src_len, tgt_len):
    def layer_step(grad_carry, layer_args):
        w_layer, query_layer, cot_layer = layer_args
        out_layer, grad_query, source_part = layer_grads(encoder_states, w_layer, query_layer, cot_layer, src_len, tgt_len)
        return grad_carry + source_part, (out_layer, grad_query)

    zero_grads = jnp.zeros((BATCH, SRC, D), jnp.float32)
    grad_source, stacked = lax.scan(layer_step, zero_grads, (w_kv, queries, cotangent))
    return stacked[0], stacked[1], grad_source.astype(jnp.bfloat16)
```

```python
import functools

import jax
import jax.numpy as jnp
from jax import lax
from jax.experimental import pallas as pl
from jax.experimental.pallas import tpu as pltpu
from jax.sharding import PartitionSpec as P


masked_score = -1e30
NT = (((1,), (1,)), ((), ()))
NN = (((1,), (0,)), ((), ()))
TN = (((0,), (0,)), ((), ()))
LAYERS = 4
CHUNKS = 2


def dot(a, b, dims):
    return lax.dot_general(a, b, dims, preferred_element_type=jnp.float32)


def low(a):
    return a.astype(jnp.bfloat16)


def wide(a):
    return a.astype(jnp.float32)


def bf(*shape):
    return jax.ShapeDtypeStruct(shape, jnp.bfloat16)


def fixed(shape):
    return pl.BlockSpec(shape, lambda i, *s: (0,) * len(shape))


def project_kernel(x_ref, w_ref, out_ref):
    out_ref[0] = low(dot(x_ref[...], w_ref[0], NN))


def project(rows, w_kv):
    layers, width, cols = w_kv.shape
    count = rows.shape[0]
    return pl.pallas_call(
        project_kernel,
        out_shape=bf(layers, count, cols),
        grid=(layers,),
        in_specs=[fixed((count, width)), pl.BlockSpec((1, width, cols), lambda r: (r, 0, 0))],
        out_specs=pl.BlockSpec((1, count, cols), lambda r: (r, 0, 0)),
        name="project",
    )(rows, w_kv)


def forward_kernel(shards, scalars, src_len, tgt_len, mine, mate, kv_ref, qc_ref, stat_ref):
    b = pl.program_id(0)
    seat, core = scalars[0], scalars[1]
    layers, keys, cols = kv_ref.shape
    head = cols // 2
    rows = qc_ref.shape[3]
    scale = head ** (-0.5)
    live = lax.broadcasted_iota(jnp.int32, (rows, head), 0) < tgt_len[b]
    key_live = seat * keys + lax.broadcasted_iota(jnp.int32, (keys, rows), 0) < src_len[b]
    first = core == 0
    tops, deltas = [], []
    for r in range(layers):
        whole = []
        for kind in range(2):
            a, c = wide(mine[r, kind, 0]), wide(mate[r, kind, 0])
            whole.append(jnp.concatenate([jnp.where(first, a, c), jnp.where(first, c, a)], axis=0))
        query, grad = low(whole[0]), low(jnp.where(live, whole[1], 0.0))
        qc_ref[0, r, 0] = query
        qc_ref[1, r, 0] = grad
        pair = kv_ref[r]
        scores = jnp.where(key_live, dot(pair[:, :head], query, NT) * scale, masked_score)
        top = jnp.max(scores, axis=0, keepdims=True)
        power = jnp.exp(scores - top)
        total = jnp.sum(power, axis=0, keepdims=True)
        part = jnp.sum(power * dot(pair[:, head:], grad, NT), axis=0, keepdims=True)
        tops.append(top + jnp.log(total))
        deltas.append(part / total)
    stats = jnp.concatenate(tops + deltas, axis=0)
    for peer in range(shards):
        stat_ref[peer, 0] = stats


def forward(shards, scalars, src_len, tgt_len, mine, mate, kv, samples):
    layers, _, _, half, head = mine.shape
    rows = 2 * half
    keys = kv.shape[1] // samples
    part = pl.BlockSpec((layers, 2, 1, half, head), lambda b, *s: (0, 0, b, 0, 0))
    return pl.pallas_call(
        functools.partial(forward_kernel, shards),
        out_shape=(
            bf(2, layers, samples, rows, head),
            jax.ShapeDtypeStruct((shards, samples, 2 * layers, rows), jnp.float32),
        ),
        grid_spec=pltpu.PrefetchScalarGridSpec(
            num_scalar_prefetch=3,
            grid=(samples,),
            in_specs=[part, part, pl.BlockSpec((layers, keys, kv.shape[2]), lambda b, *s: (0, b, 0))],
            out_specs=(
                pl.BlockSpec((2, layers, 1, rows, head), lambda b, *s: (0, 0, b, 0, 0)),
                pl.BlockSpec((shards, 1, 2 * layers, rows), lambda b, *s: (0, b, 0, 0)),
            ),
        ),
        name="forward",
    )(scalars, src_len, tgt_len, mine, mate, kv)


def backward_kernel(scalars, src_len, kv_ref, qc_ref, stat_ref, od_ref, grads):
    b = pl.program_id(0)
    seat = scalars[0]
    layers, keys, cols = kv_ref.shape
    head = cols // 2
    shards = stat_ref.shape[0]
    rows = qc_ref.shape[3]
    scale = head ** (-0.5)
    stat = stat_ref[:, 0]
    lse = stat[:, :layers]
    top = jnp.max(lse, axis=0)
    weight = jnp.exp(lse - top[None])
    inverse = 1.0 / jnp.sum(weight, axis=0)
    delta = jnp.sum(weight * stat[:, layers:], axis=0) * inverse
    limit = src_len[b]
    down_live = seat * keys + lax.broadcasted_iota(jnp.int32, (keys, rows), 0) < limit
    for r in range(layers):
        pair = kv_ref[r]
        key, value = pair[:, :head], pair[:, head:]
        query, grad = qc_ref[0, r, 0], qc_ref[1, r, 0]
        scores = jnp.where(down_live, dot(key, query, NT) * scale, masked_score)
        prob = jnp.exp(scores - top[r:r + 1, :]) * inverse[r:r + 1, :]
        slope = low(prob * (dot(value, grad, NT) - delta[r:r + 1, :]))
        prob = low(prob)
        grads[r, :, :head] = low(dot(slope, query, NN) * scale)
        grads[r, :, head:] = low(dot(prob, grad, NN))
        out = dot(prob, value, TN)
        query_grad = dot(slope, key, TN)
        od_ref[:, 0, r, 0] = low(out).reshape(shards, rows // shards, head)
        od_ref[:, 1, r, 0] = low(query_grad * scale).reshape(shards, rows // shards, head)


def backward(scalars, src_len, kv, qc, stats):
    _, layers, samples, rows, head = qc.shape
    shards = stats.shape[0]
    keys = kv.shape[1] // samples
    cols = kv.shape[2]
    pairs = pl.BlockSpec((layers, keys, cols), lambda b, *s: (0, b, 0))
    return pl.pallas_call(
        backward_kernel,
        out_shape=(bf(shards, 2, layers, samples, rows // shards, head), bf(*kv.shape)),
        grid_spec=pltpu.PrefetchScalarGridSpec(
            num_scalar_prefetch=2,
            grid=(samples,),
            in_specs=[
                pairs,
                pl.BlockSpec((2, layers, 1, rows, head), lambda b, *s: (0, 0, b, 0, 0)),
                pl.BlockSpec((shards, 1, 2 * layers, rows), lambda b, *s: (0, b, 0, 0)),
            ],
            out_specs=(
                pl.BlockSpec((shards, 2, layers, 1, rows // shards, head), lambda b, *s: (0, 0, 0, b, 0, 0)),
                pairs,
            ),
        ),
        name="backward",
    )(scalars, src_len, kv, qc, stats)


def terms_of(grads, w_ref):
    layers = grads.shape[0]
    terms = None
    for r in range(layers):
        weight = w_ref[r, 0]
        weight = weight.reshape(weight.shape[0] * weight.shape[1], weight.shape[2])
        term = dot(grads[r], weight, NT)
        terms = term if terms is None else terms + term
    return terms


def spread_kernel(scalars, grads, w_ref, up_ref, down_ref, next_ref, prev_ref):
    step = pl.program_id(0)
    terms = low(terms_of(grads, w_ref))
    half = terms.shape[0] // 2

    @pl.when(step == 0)
    def _():
        up_ref[:half] = terms[:half]
        down_ref[:half] = terms[half:]

    @pl.when(step == 1)
    def _():
        next_ref[...] = terms[:half]
        up_ref[half:] = terms[half:]

    @pl.when(step == 2)
    def _():
        down_ref[half:] = terms[:half]
        prev_ref[...] = terms[half:]


def spread(scalars, grads, w_view, chunk):
    layers, sections, heads, block, cols = w_view.shape
    count = grads.shape[1]
    part = block // CHUNKS
    outs = (bf(count, heads * part), bf(count, heads * part), bf(count // 2, heads * part), bf(count // 2, heads * part))
    return pl.pallas_call(
        spread_kernel,
        out_shape=outs,
        grid_spec=pltpu.PrefetchScalarGridSpec(
            num_scalar_prefetch=1,
            grid=(3,),
            in_specs=[
                fixed(grads.shape),
                pl.BlockSpec((layers, 1, heads, part, cols), lambda i, s: (0, s[4 + i], 0, chunk, 0)),
            ],
            out_specs=tuple(fixed(a.shape) for a in outs),
        ),
        name=f"spread{chunk}",
    )(scalars, grads, w_view)


def pass_kernel(nxt, from_down, prv, from_up, up_ref, down_ref):
    up_ref[...] = low(wide(nxt[...]) + wide(from_down[...]))
    down_ref[...] = low(wide(prv[...]) + wide(from_up[...]))


def pass_on(nxt, from_down, prv, from_up, chunk):
    return pl.pallas_call(
        pass_kernel,
        out_shape=(bf(*nxt.shape), bf(*nxt.shape)),
        grid=(1,),
        in_specs=[fixed(nxt.shape)] * 4,
        out_specs=(fixed(nxt.shape),) * 2,
        name=f"pass{chunk}",
    )(nxt, from_down, prv, from_up)


def gather_kernel(scalars, grads, w_ref, from_down, from_up, low_ref, high_ref, out_ref):
    terms = terms_of(grads, w_ref)
    half = terms.shape[0] // 2
    heads, _, part = out_ref.shape
    first = terms[:half] + wide(low_ref[...]) + wide(from_up[...])
    second = terms[half:] + wide(high_ref[...]) + wide(from_down[...])
    for h in range(heads):
        out_ref[h, :half] = low(first[:, h * part:(h + 1) * part])
        out_ref[h, half:] = low(second[:, h * part:(h + 1) * part])


def gather(scalars, grads, w_view, from_down, from_up, lower, higher, chunk):
    layers, sections, heads, block, cols = w_view.shape
    count = grads.shape[1]
    part = block // CHUNKS
    tail = pl.BlockSpec((count // 2, heads * part), lambda i, s: (1, 0))
    return pl.pallas_call(
        gather_kernel,
        out_shape=bf(heads, count, part),
        grid_spec=pltpu.PrefetchScalarGridSpec(
            num_scalar_prefetch=1,
            grid=(1,),
            in_specs=[
                fixed(grads.shape),
                pl.BlockSpec((layers, 1, heads, part, cols), lambda i, s: (0, s[7], 0, chunk, 0)),
                tail,
                tail,
                fixed(lower.shape),
                fixed(higher.shape),
            ],
            out_specs=fixed((heads, count, part)),
        ),
        name=f"gather{chunk}",
    )(scalars, grads, w_view, from_down, from_up, lower, higher)


def turn(count, by):
    return [(i, (i + by) % count) for i in range(count)]


def flip(count, bit):
    return [(i, i ^ bit) for i in range(count)]


def body(encoder_states, w_kv, queries, cotangent, src_len, tgt_len):
    sec = lax.axis_index("section")
    seat = lax.axis_index("seq")
    shards = lax.axis_size("seq")
    samples, src_rows, width = encoder_states.shape
    layers, _, cols = w_kv.shape
    head = cols // 2
    rows = queries.shape[2]
    half = rows // 2
    core = seat % 2
    places = [(sec + by) % 4 for by in (2, 1, 3, 0)]
    scalars = jnp.stack([seat, core, sec, sec, *places]).astype(jnp.int32)

    up = lambda a: lax.ppermute(a, "section", turn(4, 1))
    down = lambda a: lax.ppermute(a, "section", turn(4, 3))

    halves = [
        jnp.transpose(lax.dynamic_slice_in_dim(a[0], core * half, half, 1), (2, 0, 1, 3)) for a in (queries, cotangent)
    ]
    mine = lax.all_to_all(jnp.stack(halves, 1), "section", 0, 0, tiled=True)
    mate = lax.ppermute(mine, "seq", flip(shards, 1))
    kv = project(encoder_states.reshape(samples * src_rows, width), w_kv)
    qc, stats = forward(shards, scalars, src_len, tgt_len, mine, mate, kv, samples)
    stats = lax.all_to_all(stats, "seq", 0, 0, tiled=True)
    od, grads = backward(scalars, src_len, kv, qc, stats)

    w_view = w_kv.reshape(layers, 4, 4, width // 16, cols)
    pieces = []
    for chunk in range(CHUNKS):
        to_up, to_down, nxt, prv = spread(scalars, grads, w_view, chunk)
        from_down, from_up = up(to_up), down(to_down)
        lower, higher = pass_on(nxt, from_down, prv, from_up, chunk)
        lower, higher = up(lower), down(higher)
        joined = gather(scalars, grads, w_view, from_down, from_up, lower, higher, chunk)
        joined = lax.all_to_all(joined, "head", 0, 0, tiled=True)
        pieces.append(low(jnp.sum(wide(joined), axis=0)))
    source_grads = jnp.concatenate(pieces, axis=1).reshape(samples, src_rows, cols)

    od = lax.all_to_all(od, "seq", 0, 0, tiled=True)
    od = low(jnp.sum(wide(od), axis=0))
    od = lax.all_to_all(jnp.transpose(od, (1, 0, 2, 3, 4)), "section", 0, 0, tiled=True)
    od = jnp.transpose(od, (1, 2, 3, 0, 4))
    return od[0][None], od[1][None], source_grads


def solution(mesh):
    placed = (
        P(None, "seq", None),
        P(None, None, ("section", "head")),
        P("section", None, None, None, "head"),
        P("section", None, None, None, "head"),
        P(),
        P(),
    )
    return jax.shard_map(
        body,
        mesh=mesh,
        in_specs=placed,
        out_specs=(
            P("section", None, "seq", None, "head"),
            P("section", None, "seq", None, "head"),
            P(None, "seq", ("section", "head")),
        ),
        check_vma=False,
    )
```

```python
import functools

import jax
import jax.numpy as jnp
from jax import lax
from jax.experimental import pallas as pl
from jax.experimental.pallas import tpu as pltpu
from jax.sharding import PartitionSpec as P


masked_score = -1e30
NT = (((1,), (1,)), ((), ()))
NN = (((1,), (0,)), ((), ()))
TN = (((0,), (0,)), ((), ()))
CHUNKS = 2


def dot(a, b, dims):
    return lax.dot_general(a, b, dims, preferred_element_type=jnp.float32)


def low(a):
    return a.astype(jnp.bfloat16)


def wide(a):
    return a.astype(jnp.float32)


def bf(*shape):
    return jax.ShapeDtypeStruct(shape, jnp.bfloat16)


def fixed(shape):
    return pl.BlockSpec(shape, lambda i, *s: (0,) * len(shape))


def project_kernel(x_ref, w_ref, out_ref):
    out_ref[0] = low(dot(x_ref[...], w_ref[0], NN))


def project(rows, w_kv):
    layers, width, cols = w_kv.shape
    count = rows.shape[0]
    return pl.pallas_call(
        project_kernel,
        out_shape=bf(layers, count, cols),
        grid=(layers,),
        in_specs=[fixed((count, width)), pl.BlockSpec((1, width, cols), lambda r: (r, 0, 0))],
        out_specs=pl.BlockSpec((1, count, cols), lambda r: (r, 0, 0)),
        name="project",
    )(rows, w_kv)


def forward_kernel(shards, scalars, src_len, tgt_len, mine, mate, kv_ref, qc_ref, stat_ref):
    b = pl.program_id(0)
    seat, core = scalars[0], scalars[1]
    layers, keys, cols = kv_ref.shape
    head = cols // 2
    rows = qc_ref.shape[3]
    scale = head ** (-0.5)
    live = lax.broadcasted_iota(jnp.int32, (rows, head), 0) < tgt_len[b]
    key_live = seat * keys + lax.broadcasted_iota(jnp.int32, (keys, rows), 0) < src_len[b]
    first = core == 0
    tops, deltas = [], []
    for r in range(layers):
        whole = []
        for kind in range(2):
            a, c = wide(mine[r, kind, 0]), wide(mate[r, kind, 0])
            whole.append(jnp.concatenate([jnp.where(first, a, c), jnp.where(first, c, a)], axis=0))
        query, grad = low(whole[0]), low(jnp.where(live, whole[1], 0.0))
        qc_ref[0, r, 0] = query
        qc_ref[1, r, 0] = grad
        pair = kv_ref[r]
        scores = jnp.where(key_live, dot(pair[:, :head], query, NT) * scale, masked_score)
        top = jnp.max(scores, axis=0, keepdims=True)
        power = jnp.exp(scores - top)
        total = jnp.sum(power, axis=0, keepdims=True)
        part = jnp.sum(power * dot(pair[:, head:], grad, NT), axis=0, keepdims=True)
        tops.append(top + jnp.log(total))
        deltas.append(part / total)
    stats = jnp.concatenate(tops + deltas, axis=0)
    for peer in range(shards):
        stat_ref[peer, 0] = stats


def forward(shards, scalars, src_len, tgt_len, mine, mate, kv, samples):
    layers, _, _, half, head = mine.shape
    rows = 2 * half
    keys = kv.shape[1] // samples
    part = pl.BlockSpec((layers, 2, 1, half, head), lambda b, *s: (0, 0, b, 0, 0))
    return pl.pallas_call(
        functools.partial(forward_kernel, shards),
        out_shape=(
            bf(2, layers, samples, rows, head),
            jax.ShapeDtypeStruct((shards, samples, 2 * layers, rows), jnp.float32),
        ),
        grid_spec=pltpu.PrefetchScalarGridSpec(
            num_scalar_prefetch=3,
            grid=(samples,),
            in_specs=[part, part, pl.BlockSpec((layers, keys, kv.shape[2]), lambda b, *s: (0, b, 0))],
            out_specs=(
                pl.BlockSpec((2, layers, 1, rows, head), lambda b, *s: (0, 0, b, 0, 0)),
                pl.BlockSpec((shards, 1, 2 * layers, rows), lambda b, *s: (0, b, 0, 0)),
            ),
        ),
        name="forward",
    )(scalars, src_len, tgt_len, mine, mate, kv)


def backward_kernel(samples, scalars, src_len, kv_ref, qc_ref, stat_ref, w_ref, keep_ref, give_ref, grads_ref, *rest):
    far_refs, grads = rest[:-1], rest[-1]
    step = pl.program_id(0)
    layers, keys, cols = kv_ref.shape
    head = cols // 2
    shards = stat_ref.shape[0]
    rows = qc_ref.shape[3]
    scale = head ** (-0.5)

    @pl.when(step < samples)
    def _():
        seat = scalars[0]
        even = scalars[1] == 0
        stat = stat_ref[:, 0]
        lse = stat[:, :layers]
        top = jnp.max(lse, axis=0)
        weight = jnp.exp(lse - top[None])
        inverse = 1.0 / jnp.sum(weight, axis=0)
        delta = jnp.sum(weight * stat[:, layers:], axis=0) * inverse
        limit = src_len[jnp.minimum(step, samples - 1)]
        down_live = seat * keys + lax.broadcasted_iota(jnp.int32, (keys, rows), 0) < limit
        at = pl.ds(pl.multiple_of(step * keys, keys), keys)
        for r in range(layers):
            pair = kv_ref[r]
            key, value = pair[:, :head], pair[:, head:]
            query, grad = qc_ref[0, r, 0], qc_ref[1, r, 0]
            scores = jnp.where(down_live, dot(key, query, NT) * scale, masked_score)
            prob = jnp.exp(scores - top[r:r + 1, :]) * inverse[r:r + 1, :]
            slope = low(prob * (dot(value, grad, NT) - delta[r:r + 1, :]))
            prob = low(prob)
            both = jnp.concatenate([low(dot(slope, query, NN) * scale), low(dot(prob, grad, NN))], axis=1)
            grads_ref[r] = both
            grads[r, at, :] = both
            out = dot(prob, value, TN)
            query_grad = dot(slope, key, TN)
            for kind, value in enumerate((out, query_grad * scale)):
                value = value.reshape(shards // 2, 2, rows // shards, head)
                keep_ref[:, kind, r, 0] = low(jnp.where(even, value[:, 0], value[:, 1]))
                give_ref[:, kind, r, 0] = low(jnp.where(even, value[:, 1], value[:, 0]))

    @pl.when(step == samples)
    def _():
        terms = low(terms_of(grads, w_ref))
        size = far_refs[0].shape[0]
        for k, ref in enumerate(far_refs):
            ref[...] = terms[k * size:(k + 1) * size]


def backward(scalars, src_len, kv, qc, stats, w_view):
    _, layers, samples, rows, head = qc.shape
    shards = stats.shape[0]
    keys = kv.shape[1] // samples
    cols = kv.shape[2]
    part = w_view.shape[2]
    at = lambda i: jnp.minimum(i, samples - 1)
    pairs = pl.BlockSpec((layers, keys, cols), lambda i, *s: (0, at(i), 0))
    far = bf(kv.shape[1] // (2 * CHUNKS), part)
    return pl.pallas_call(
        functools.partial(backward_kernel, samples),
        out_shape=(bf(shards // 2, 2, layers, samples, rows // shards, head),) * 2 + (bf(*kv.shape),) + (far,) * (2 * CHUNKS),
        grid_spec=pltpu.PrefetchScalarGridSpec(
            num_scalar_prefetch=2,
            grid=(samples + 1,),
            in_specs=[
                pairs,
                pl.BlockSpec((2, layers, 1, rows, head), lambda i, *s: (0, 0, at(i), 0, 0)),
                pl.BlockSpec((shards, 1, 2 * layers, rows), lambda i, *s: (0, at(i), 0, 0)),
                pl.BlockSpec((layers, 1, part, cols), lambda i, s, n: (0, s[4], 0, 0)),
            ],
            out_specs=(
                pl.BlockSpec((shards // 2, 2, layers, 1, rows // shards, head), lambda i, *s: (0, 0, 0, at(i), 0, 0)),
            ) * 2 + (pairs,) + (fixed(far.shape),) * (2 * CHUNKS),
            scratch_shapes=[pltpu.VMEM(kv.shape, jnp.bfloat16)],
        ),
        name="backward",
    )(scalars, src_len, kv, qc, stats, w_view)


def terms_of(grads, w_ref):
    terms = None
    for r in range(grads.shape[0]):
        term = dot(grads[r], w_ref[r, 0], NT)
        terms = term if terms is None else terms + term
    return terms


def near_kernel(scalars, grads, w_ref, *outs):
    step = pl.program_id(0)
    terms = low(terms_of(grads, w_ref))
    size = outs[0].shape[0]
    for side in range(2):
        @pl.when(step == side)
        def _():
            for k in range(CHUNKS):
                outs[side * CHUNKS + k][...] = terms[k * size:(k + 1) * size]


def near(scalars, grads, w_view):
    layers, _, part, cols = w_view.shape
    out = bf(grads.shape[1] // CHUNKS, part)
    return pl.pallas_call(
        near_kernel,
        out_shape=(out,) * (2 * CHUNKS),
        grid_spec=pltpu.PrefetchScalarGridSpec(
            num_scalar_prefetch=1,
            grid=(2,),
            in_specs=[fixed(grads.shape), pl.BlockSpec((layers, 1, part, cols), lambda i, s: (0, s[5 + i], 0, 0))],
            out_specs=(fixed(out.shape),) * (2 * CHUNKS),
        ),
        name="near",
    )(scalars, grads, w_view)


def here_kernel(scalars, grads, w_ref, out_ref):
    out_ref[...] = low(terms_of(grads, w_ref))


def here(scalars, grads, w_view):
    layers, _, part, cols = w_view.shape
    count = grads.shape[1]
    block = part // 2
    return pl.pallas_call(
        here_kernel,
        out_shape=bf(count, part),
        grid_spec=pltpu.PrefetchScalarGridSpec(
            num_scalar_prefetch=1,
            grid=(2,),
            in_specs=[fixed(grads.shape), pl.BlockSpec((layers, 1, block, cols), lambda i, s: (0, s[7], i, 0))],
            out_specs=pl.BlockSpec((count, block), lambda i, s: (0, i)),
        ),
        name="here",
    )(scalars, grads, w_view)


def halve_kernel(scalars, keep_a, keep_b, give_a, give_b, keep_ref, give_ref):
    keep_ref[...] = low(wide(keep_a[...]) + wide(keep_b[...]))
    give_ref[...] = low(wide(give_a[...]) + wide(give_b[...]))


def halve(scalars, kept, came, bit):
    count = kept.shape[0] // 2
    tail = kept.shape[1:]
    view = (count, 2) + tail
    kept, came = kept.reshape(view), came.reshape(view)
    nothing = (0,) * len(tail)
    mine = pl.BlockSpec((1, pl.squeezed) + tail, lambda i, s: (i, s[8 + bit]) + nothing)
    other = pl.BlockSpec((1, pl.squeezed) + tail, lambda i, s: (i, 1 - s[8 + bit]) + nothing)
    out = pl.BlockSpec((1,) + tail, lambda i, s: (i,) + nothing)
    return pl.pallas_call(
        halve_kernel,
        out_shape=(bf(count, *tail),) * 2,
        grid_spec=pltpu.PrefetchScalarGridSpec(
            num_scalar_prefetch=1, grid=(count,), in_specs=[mine, mine, other, other], out_specs=(out, out)
        ),
    )(scalars, kept, came, kept, came)


def deal_kernel(scalars, kept, came, *outs):
    sec = scalars[2]
    for k, ref in enumerate(outs):
        layer = lax.rem(sec + k, len(outs))
        ref[...] = low(wide(kept[0, :, layer]) + wide(came[0, :, layer]))


def deal(scalars, kept, came):
    _, kinds, layers, samples, rows, head = kept.shape
    out = bf(kinds, samples, rows, head)
    return pl.pallas_call(
        deal_kernel,
        out_shape=(out,) * layers,
        grid_spec=pltpu.PrefetchScalarGridSpec(
            num_scalar_prefetch=1,
            grid=(1,),
            in_specs=[fixed(kept.shape)] * 2,
            out_specs=(fixed(out.shape),) * layers,
        ),
        name="deal",
    )(scalars, kept, came)


def pass_kernel(up_in, down_in, from_down, from_up, up_ref, down_ref):
    up_ref[...] = low(wide(up_in[...]) + wide(from_down[...]))
    down_ref[...] = low(wide(down_in[...]) + wide(from_up[...]))


def pass_on(up_in, down_in, from_down, from_up):
    half, width = from_down.shape
    block = (half, width // 2)
    top = pl.BlockSpec(block, lambda i: (0, i))
    bottom = pl.BlockSpec(block, lambda i: (1, i))
    return pl.pallas_call(
        pass_kernel,
        out_shape=(bf(*up_in.shape), bf(*up_in.shape)),
        grid=(2,),
        in_specs=[top, bottom, top, top],
        out_specs=(top, bottom),
        input_output_aliases={0: 0, 1: 1},
    )(up_in, down_in, from_down, from_up)


def gather_kernel(own, from_down, from_up, out_ref):
    out_ref[0] = low(wide(own[...]) + wide(from_down[...]) + wide(from_up[...]))


def gather(own, from_down, from_up, heads, chunk):
    count, width = from_down.shape
    part = width // heads
    block = pl.BlockSpec((count, part), lambda h: (0, h))
    return pl.pallas_call(
        gather_kernel,
        out_shape=bf(heads, count, part),
        grid=(heads,),
        in_specs=[pl.BlockSpec((count, part), lambda h: (chunk, h)), block, block],
        out_specs=pl.BlockSpec((1, count, part), lambda h: (h, 0, 0)),
    )(own, from_down, from_up)


def turn(count, by):
    return [(i, (i + by) % count) for i in range(count)]


def flip(count, bit):
    return [(i, i ^ bit) for i in range(count)]


def body(encoder_states, w_kv, queries, cotangent, src_len, tgt_len):
    sec = lax.axis_index("section")
    seat = lax.axis_index("seq")
    shards = lax.axis_size("seq")
    samples, src_rows, width = encoder_states.shape
    layers, _, cols = w_kv.shape
    rows = queries.shape[2]
    half = rows // 2
    core = seat % 2
    places = [(sec + by) % 4 for by in (2, 1, 3, 0)]
    bits = [(seat // (1 << k)) % 2 for k in range(4)]
    scalars = jnp.stack([seat, core, sec, sec, *places, *bits]).astype(jnp.int32)

    def up(a):
        return lax.ppermute(a, "section", turn(4, 1))

    def down(a):
        return lax.ppermute(a, "section", turn(4, 3))

    def swap(a, axis):
        return lax.all_to_all(a, axis, 0, 0, tiled=True)

    halves = [
        jnp.transpose(lax.dynamic_slice_in_dim(a[0], core * half, half, 1), (2, 0, 1, 3)) for a in (queries, cotangent)
    ]
    mine = swap(jnp.stack(halves, 1), "section")
    kv = project(encoder_states.reshape(samples * src_rows, width), w_kv)
    mine, kv = lax.optimization_barrier((mine, kv))
    mate = lax.ppermute(mine, "seq", flip(shards, 1))
    qc, stats = forward(shards, scalars, src_len, tgt_len, mine, mate, kv, samples)
    stats = swap(stats, "seq")

    sections, heads = lax.axis_size("section"), lax.axis_size("head")
    w_view = w_kv.reshape(layers, sections, width // sections, cols)
    kept, give, grads, *far = backward(scalars, src_len, kv, qc, stats, w_view)
    passed = [(up(far[2 * c]), down(far[2 * c + 1])) for c in range(CHUNKS)]
    sides = near(scalars, grads, w_view)
    own = here(scalars, grads, w_view)
    pieces = []
    for c in range(CHUNKS):
        to_up, to_down = pass_on(sides[c], sides[CHUNKS + c], *passed[c])
        to_up, to_down = up(to_up), down(to_down)
        joined = gather(own, to_up, to_down, heads, c)
        joined = swap(joined, "head")
        pieces.append(low(jnp.sum(wide(joined), axis=0)))
    source_grads = jnp.concatenate(pieces).reshape(samples, src_rows, cols)

    for bit in range(4):
        came = lax.ppermute(give, "seq", flip(shards, 1 << bit))
        if bit < 3:
            kept, give = halve(scalars, kept, came, bit + 1)
    own, to_up, to_far, to_down = deal(scalars, kept, came)
    from_down, from_up = up(to_up), down(to_down)
    from_far = lax.ppermute(to_far, "section", turn(4, 2))
    ring = jnp.stack([own, from_down, from_far, from_up])
    groups = [lax.dynamic_index_in_dim(ring, (sec + 4 - g) % 4, 0, keepdims=False) for g in range(4)]
    od = jnp.stack(groups, axis=3)
    return od[0][None], od[1][None], source_grads


def solution(mesh):
    placed = (
        P(None, "seq", None),
        P(None, None, ("section", "head")),
        P("section", None, None, None, "head"),
        P("section", None, None, None, "head"),
        P(),
        P(),
    )

    return jax.shard_map(
        body,
        mesh=mesh,
        in_specs=placed,
        out_specs=(
            P("section", None, "seq", None, "head"),
            P("section", None, "seq", None, "head"),
            P(None, "seq", ("section", "head")),
        ),
        check_vma=False,
    )
```

```python
import functools

import jax
import jax.numpy as jnp
from jax import lax
from jax.experimental import pallas as pl
from jax.experimental.pallas import tpu as pltpu
from jax.sharding import PartitionSpec as P


masked_score = -1e30
NT = (((1,), (1,)), ((), ()))
NN = (((1,), (0,)), ((), ()))
TN = (((0,), (0,)), ((), ()))
CHUNKS = 2


def dot(a, b, dims):
    return lax.dot_general(a, b, dims, preferred_element_type=jnp.float32)


def low(a):
    return a.astype(jnp.bfloat16)


def wide(a):
    return a.astype(jnp.float32)


def bf(*shape):
    return jax.ShapeDtypeStruct(shape, jnp.bfloat16)


def kept_here(*shape, dtype=jnp.bfloat16):
    return pltpu.VMEM(shape, dtype)


def held(*arrays):
    return [pltpu.with_memory_space_constraint(a, pltpu.VMEM) for a in arrays]


def in_hbm(array):
    return pltpu.with_memory_space_constraint(array, pltpu.HBM)


ROOM = pltpu.CompilerParams(vmem_limit_bytes=16 * 1024 * 1024)
FAST = pl.BlockSpec(memory_space=pltpu.VMEM)
SLOW = pl.BlockSpec(memory_space=pl.ANY)
SCALAR = pl.BlockSpec(memory_space=pltpu.SMEM)


def project_kernel(x_ref, w_ref, out_ref):
    out_ref[pl.program_id(0)] = low(dot(x_ref[...], w_ref[0], NN))


def project(rows, w_kv):
    layers, width, cols = w_kv.shape
    count = rows.shape[0]
    return pl.pallas_call(
        project_kernel,
        out_shape=kept_here(layers, count, cols),
        grid=(layers,),
        in_specs=[
            pl.BlockSpec((count, width), lambda r: (0, 0)),
            pl.BlockSpec((1, width, cols), lambda r: (r, 0, 0)),
        ],
        out_specs=FAST,
        compiler_params=ROOM,
        name="project",
    )(in_hbm(rows), in_hbm(w_kv))


def forward_kernel(scalars, src_len, tgt_len, mine, mate, kv_ref, qc_ref, stat_ref):
    seat, core = scalars[0], scalars[1]
    layers, count, _ = kv_ref.shape
    _, _, samples, rows, head = qc_ref.shape
    shards = stat_ref.shape[0]
    keys = count // samples
    scale = head ** (-0.5)
    first = core == 0

    def one(b, carry):
        live = lax.broadcasted_iota(jnp.int32, (rows, head), 0) < tgt_len[b]
        key_live = seat * keys + lax.broadcasted_iota(jnp.int32, (keys, rows), 0) < src_len[b]
        tops, deltas = [], []
        for r in range(layers):
            whole = []
            for kind in range(2):
                a, c = wide(mine[r, kind, b]), wide(mate[r, kind, b])
                whole.append(jnp.concatenate([jnp.where(first, a, c), jnp.where(first, c, a)], axis=0))
            query, grad = low(whole[0]), low(jnp.where(live, whole[1], 0.0))
            qc_ref[0, r, b] = query
            qc_ref[1, r, b] = grad
            pair = kv_ref[r, pl.ds(pl.multiple_of(b * keys, keys), keys), :]
            scores = jnp.where(key_live, dot(pair[:, :head], query, NT) * scale, masked_score)
            top = jnp.max(scores, axis=0, keepdims=True)
            power = jnp.exp(scores - top)
            total = jnp.sum(power, axis=0, keepdims=True)
            part = jnp.sum(power * dot(pair[:, head:], grad, NT), axis=0, keepdims=True)
            tops.append(top + jnp.log(total))
            deltas.append(part / total)
        stats = jnp.concatenate(tops + deltas, axis=0)
        for peer in range(shards):
            stat_ref[peer, b] = stats
        return carry

    lax.fori_loop(0, samples, one, 0)


def forward(shards, scalars, src_len, tgt_len, mine, mate, kv):
    layers, _, samples, half, head = mine.shape
    rows = 2 * half
    return pl.pallas_call(
        forward_kernel,
        out_shape=(
            kept_here(2, layers, samples, rows, head),
            kept_here(shards, samples, 2 * layers, rows, dtype=jnp.float32),
        ),
        in_specs=[SCALAR] * 3 + [FAST] * 3,
        out_specs=(FAST, FAST),
        compiler_params=ROOM,
        name="forward",
    )(scalars, src_len, tgt_len, *held(mine, mate, kv))


def terms_of(grads, w_ref, place, part):
    terms = None
    at = pl.ds(pl.multiple_of(place * part, part), part)
    for r in range(grads.shape[0]):
        term = dot(grads[r], w_ref[r, at, :], NT)
        terms = term if terms is None else terms + term
    return terms


def backward_kernel(scalars, src_len, kv_ref, qc_ref, stat_ref, w_hbm, keep_ref, give_ref, grads, w_ref, *rest):
    far_refs, w_sem = rest[:-1], rest[-1]
    take = pltpu.make_async_copy(w_hbm, w_ref, w_sem)
    take.start()
    layers, count, _ = kv_ref.shape
    _, _, samples, rows, head = qc_ref.shape
    shards = stat_ref.shape[0]
    keys = count // samples
    scale = head ** (-0.5)
    seat = scalars[0]
    even = scalars[1] == 0

    def one(b, carry):
        stat = stat_ref[:, b]
        lse = stat[:, :layers]
        top = jnp.max(lse, axis=0)
        weight = jnp.exp(lse - top[None])
        inverse = 1.0 / jnp.sum(weight, axis=0)
        delta = jnp.sum(weight * stat[:, layers:], axis=0) * inverse
        down_live = seat * keys + lax.broadcasted_iota(jnp.int32, (keys, rows), 0) < src_len[b]
        at = pl.ds(pl.multiple_of(b * keys, keys), keys)
        for r in range(layers):
            pair = kv_ref[r, at, :]
            key, value = pair[:, :head], pair[:, head:]
            query, grad = qc_ref[0, r, b], qc_ref[1, r, b]
            scores = jnp.where(down_live, dot(key, query, NT) * scale, masked_score)
            prob = jnp.exp(scores - top[r:r + 1, :]) * inverse[r:r + 1, :]
            slope = low(prob * (dot(value, grad, NT) - delta[r:r + 1, :]))
            prob = low(prob)
            grads[r, at, :head] = low(dot(slope, query, NN) * scale)
            grads[r, at, head:] = low(dot(prob, grad, NN))
            for kind, out in enumerate((dot(prob, value, TN), dot(slope, key, TN) * scale)):
                out = out.reshape(shards // 2, 2, rows // shards, head)
                keep_ref[:, kind, r, b] = low(jnp.where(even, out[:, 0], out[:, 1]))
                give_ref[:, kind, r, b] = low(jnp.where(even, out[:, 1], out[:, 0]))
        return carry

    lax.fori_loop(0, samples, one, 0)
    take.wait()
    terms = low(terms_of(grads, w_ref, scalars[4], w_ref.shape[1] // 4))
    size = far_refs[0].shape[0]
    for k, ref in enumerate(far_refs):
        ref[...] = terms[k * size:(k + 1) * size]


def backward(scalars, src_len, kv, qc, stats, weights):
    _, layers, samples, rows, head = qc.shape
    shards = stats.shape[0]
    part = weights.shape[1] // 4
    half = kept_here(shards // 2, 2, layers, samples, rows // shards, head)
    far = kept_here(kv.shape[1] // (2 * CHUNKS), part)
    outs = (half, half, kept_here(*kv.shape), kept_here(*weights.shape)) + (far,) * (2 * CHUNKS)
    return pl.pallas_call(
        backward_kernel,
        out_shape=outs,
        in_specs=[SCALAR] * 2 + [FAST] * 3 + [SLOW],
        out_specs=(FAST,) * len(outs),
        scratch_shapes=[pltpu.SemaphoreType.DMA],
        compiler_params=ROOM,
        name="backward",
    )(scalars, src_len, *held(kv, qc, stats), in_hbm(weights))


def near_kernel(scalars, grads, w_ref, *outs):
    size = outs[0].shape[0]
    for side in range(2):
        terms = low(terms_of(grads, w_ref, scalars[5 + side], w_ref.shape[1] // 4))
        for k in range(CHUNKS):
            outs[side * CHUNKS + k][...] = terms[k * size:(k + 1) * size]


def near(scalars, grads, weights):
    outs = (kept_here(grads.shape[1] // CHUNKS, weights.shape[1] // 4),) * (2 * CHUNKS)
    return pl.pallas_call(
        near_kernel, out_shape=outs, in_specs=[SCALAR, FAST, FAST], out_specs=(FAST,) * len(outs), compiler_params=ROOM, name="near"
    )(scalars, *held(grads, weights))


def here_kernel(scalars, grads, w_ref, out_ref):
    out_ref[...] = low(terms_of(grads, w_ref, scalars[7], w_ref.shape[1] // 4))


def here(scalars, grads, weights):
    return pl.pallas_call(
        here_kernel,
        out_shape=kept_here(grads.shape[1], weights.shape[1] // 4),
        in_specs=[SCALAR, FAST, FAST],
        out_specs=FAST,
        compiler_params=ROOM,
        name="here",
    )(scalars, *held(grads, weights))


def halve_kernel(side, kept, came, keep_ref, give_ref):
    count = keep_ref.shape[0]
    mine = pl.ds(side[0] * count, count)
    other = pl.ds((1 - side[0]) * count, count)
    keep_ref[...] = low(wide(kept[mine]) + wide(came[mine]))
    give_ref[...] = low(wide(kept[other]) + wide(came[other]))


def halve(side, kept, came):
    out = kept_here(kept.shape[0] // 2, *kept.shape[1:])
    return pl.pallas_call(
        halve_kernel, out_shape=(out, out), in_specs=[SCALAR, FAST, FAST], out_specs=(FAST, FAST), compiler_params=ROOM
    )(side.reshape(1), *held(kept, came))


def deal_kernel(scalars, kept, came, *outs):
    for k, ref in enumerate(outs):
        layer = lax.rem(scalars[2] + k, len(outs))
        ref[...] = low(wide(kept[0, :, layer]) + wide(came[0, :, layer]))


def deal(scalars, kept, came):
    _, kinds, layers, samples, rows, head = kept.shape
    outs = (kept_here(kinds, samples, rows, head),) * layers
    return pl.pallas_call(
        deal_kernel, out_shape=outs, in_specs=[SCALAR, FAST, FAST], out_specs=(FAST,) * layers, compiler_params=ROOM, name="deal"
    )(scalars, *held(kept, came))


def pass_kernel(up_in, down_in, from_down, from_up, up_ref, down_ref):
    half = from_down.shape[0]
    up_ref[:half] = low(wide(up_in[:half]) + wide(from_down[...]))
    down_ref[half:] = low(wide(down_in[half:]) + wide(from_up[...]))
    up_ref[half:] = up_in[half:]
    down_ref[:half] = down_in[:half]


def pass_on(up_in, down_in, from_down, from_up):
    out = kept_here(*up_in.shape)
    return pl.pallas_call(
        pass_kernel, out_shape=(out, out), in_specs=[FAST] * 4, out_specs=(FAST, FAST), compiler_params=ROOM
    )(*held(up_in, down_in, from_down, from_up))


def gather_kernel(chunk, own, from_down, from_up, out_ref):
    heads, count, part = out_ref.shape
    for h in range(heads):
        at = slice(h * part, (h + 1) * part)
        mine = own[chunk * count:(chunk + 1) * count, at]
        out_ref[h] = low(wide(mine) + wide(from_down[:, at]) + wide(from_up[:, at]))


def gather(own, from_down, from_up, heads, chunk):
    count, width = from_down.shape
    return pl.pallas_call(
        functools.partial(gather_kernel, chunk),
        out_shape=kept_here(heads, count, width // heads),
        in_specs=[FAST] * 3,
        out_specs=FAST,
        compiler_params=ROOM,
    )(*held(own, from_down, from_up))


def finish_kernel(*refs):
    out_ref = refs[-1]
    count = out_ref.shape[0] // (len(refs) - 1)
    for c, ref in enumerate(refs[:-1]):
        total = wide(ref[0])
        for h in range(1, ref.shape[0]):
            total = total + wide(ref[h])
        out_ref[c * count:(c + 1) * count] = low(total)


def finish(pieces):
    _, count, part = pieces[0].shape
    return pl.pallas_call(
        finish_kernel,
        out_shape=bf(count * len(pieces), part),
        in_specs=[FAST] * len(pieces),
        out_specs=FAST,
        compiler_params=ROOM,
        name="finish",
    )(*held(*pieces))


def turn(count, by):
    return [(i, (i + by) % count) for i in range(count)]


def flip(count, bit):
    return [(i, i ^ bit) for i in range(count)]


def body(encoder_states, w_kv, queries, cotangent, src_len, tgt_len):
    sec = lax.axis_index("section")
    seat = lax.axis_index("seq")
    shards = lax.axis_size("seq")
    samples, src_rows, width = encoder_states.shape
    _, _, cols = w_kv.shape
    rows = queries.shape[2]
    half = rows // 2
    core = seat % 2
    places = [(sec + by) % 4 for by in (2, 1, 3, 0)]
    bits = [(seat // (1 << k)) % 2 for k in range(4)]
    scalars = jnp.stack([seat, core, sec, sec, *places, *bits]).astype(jnp.int32)

    def up(a):
        return lax.ppermute(a, "section", turn(4, 1))

    def down(a):
        return lax.ppermute(a, "section", turn(4, 3))

    def swap(a, axis):
        return lax.all_to_all(a, axis, 0, 0, tiled=True)

    halves = [
        jnp.transpose(lax.dynamic_slice_in_dim(a[0], core * half, half, 1), (2, 0, 1, 3)) for a in (queries, cotangent)
    ]
    mine = swap(jnp.stack(halves, 1), "section")
    kv = project(encoder_states.reshape(samples * src_rows, width), w_kv)
    mine, kv = lax.optimization_barrier((mine, kv))
    mate = lax.ppermute(mine, "seq", flip(shards, 1))
    qc, stats = forward(shards, scalars, src_len, tgt_len, mine, mate, kv)
    stats = swap(stats, "seq")

    heads = lax.axis_size("head")
    kept, give, grads, weights, *far = backward(scalars, src_len, kv, qc, stats, w_kv)
    passed = [(up(far[2 * c]), down(far[2 * c + 1])) for c in range(CHUNKS)]
    sides = near(scalars, grads, weights)
    own = here(scalars, grads, weights)
    pieces = []
    for c in range(CHUNKS):
        to_up, to_down = pass_on(sides[c], sides[CHUNKS + c], *passed[c])
        to_up, to_down = up(to_up), down(to_down)
        joined = gather(own, to_up, to_down, heads, c)
        pieces.append(swap(joined, "head"))
    source_grads = finish(pieces).reshape(samples, src_rows, cols)

    for stage, bit in enumerate((0, 3, 2, 1)):
        if stage:
            kept, give = halve(bits[bit].astype(jnp.int32), kept, came)
        came = lax.ppermute(give, "seq", flip(shards, 1 << bit))
    own, to_up, to_far, to_down = deal(scalars, kept, came)
    from_down, from_up = up(to_up), down(to_down)
    from_far = lax.ppermute(to_far, "section", turn(4, 2))
    ring = jnp.stack([own, from_down, from_far, from_up])
    groups = [lax.dynamic_index_in_dim(ring, (sec + 4 - g) % 4, 0, keepdims=False) for g in range(4)]
    od = jnp.stack(groups, axis=3)
    return od[0][None], od[1][None], source_grads


def solution(mesh):
    placed = (
        P(None, "seq", None),
        P(None, None, ("section", "head")),
        P("section", None, None, None, "head"),
        P("section", None, None, None, "head"),
        P(),
        P(),
    )

    return jax.shard_map(
        body,
        mesh=mesh,
        in_specs=placed,
        out_specs=(
            P("section", None, "seq", None, "head"),
            P("section", None, "seq", None, "head"),
            P(None, "seq", ("section", "head")),
        ),
        check_vma=False,
    )
```

```python
import functools

import jax
import jax.numpy as jnp
from jax import lax
from jax.experimental import pallas as pl
from jax.experimental.pallas import tpu as pltpu
from jax.sharding import PartitionSpec as P


masked_score = -1e30
NT = (((1,), (1,)), ((), ()))
NN = (((1,), (0,)), ((), ()))
TN = (((0,), (0,)), ((), ()))
CHUNKS = 2


def dot(a, b, dims):
    return lax.dot_general(a, b, dims, preferred_element_type=jnp.float32)


def low(a):
    return a.astype(jnp.bfloat16)


def wide(a):
    return a.astype(jnp.float32)


def bf(*shape):
    return jax.ShapeDtypeStruct(shape, jnp.bfloat16)


def kept_here(*shape, dtype=jnp.bfloat16):
    return pltpu.VMEM(shape, dtype)


def held(*arrays):
    return [pltpu.with_memory_space_constraint(a, pltpu.VMEM) for a in arrays]


def in_hbm(array):
    return pltpu.with_memory_space_constraint(array, pltpu.HBM)


ROOM = pltpu.CompilerParams(vmem_limit_bytes=16 * 1024 * 1024)
FAST = pl.BlockSpec(memory_space=pltpu.VMEM)
SLOW = pl.BlockSpec(memory_space=pl.ANY)
SCALAR = pl.BlockSpec(memory_space=pltpu.SMEM)


def project_kernel(x_ref, w_ref, out_ref):
    out_ref[pl.program_id(0)] = low(dot(x_ref[...], w_ref[0], NN))


def project(rows, w_kv):
    layers, width, cols = w_kv.shape
    count = rows.shape[0]
    return pl.pallas_call(
        project_kernel,
        out_shape=kept_here(layers, count, cols),
        grid=(layers,),
        in_specs=[
            pl.BlockSpec((count, width), lambda r: (0, 0)),
            pl.BlockSpec((1, width, cols), lambda r: (r, 0, 0)),
        ],
        out_specs=FAST,
        compiler_params=ROOM,
        name="project",
    )(in_hbm(rows), in_hbm(w_kv))


def forward_kernel(start, scalars, src_len, tgt_len, mine, mate, kv_ref, qc_ref, stat_ref):
    seat, core = scalars[0], scalars[1]
    layers, count, _ = kv_ref.shape
    _, _, samples, rows, head = qc_ref.shape
    shards = stat_ref.shape[0]
    keys = count // mine.shape[2]
    scale = head ** (-0.5)
    first = core == 0

    def one(at, carry):
        b = start + at
        live = lax.broadcasted_iota(jnp.int32, (rows, head), 0) < tgt_len[b]
        key_live = seat * keys + lax.broadcasted_iota(jnp.int32, (keys, rows), 0) < src_len[b]
        tops, deltas = [], []
        for r in range(layers):
            whole = []
            for kind in range(2):
                a, c = wide(mine[r, kind, b]), wide(mate[r, kind, b])
                whole.append(jnp.concatenate([jnp.where(first, a, c), jnp.where(first, c, a)], axis=0))
            query, grad = low(whole[0]), low(jnp.where(live, whole[1], 0.0))
            qc_ref[0, r, at] = query
            qc_ref[1, r, at] = grad
            pair = kv_ref[r, pl.ds(pl.multiple_of(b * keys, keys), keys), :]
            scores = jnp.where(key_live, dot(pair[:, :head], query, NT) * scale, masked_score)
            top = jnp.max(scores, axis=0, keepdims=True)
            power = jnp.exp(scores - top)
            total = jnp.sum(power, axis=0, keepdims=True)
            part = jnp.sum(power * dot(pair[:, head:], grad, NT), axis=0, keepdims=True)
            tops.append(top + jnp.log(total))
            deltas.append(part / total)
        stats = jnp.concatenate(tops + deltas, axis=0)
        for peer in range(shards):
            stat_ref[peer, at] = stats
        return carry

    lax.fori_loop(0, samples, one, 0)


def forward(chunk, shards, scalars, src_len, tgt_len, mine, mate, kv):
    layers, _, samples, half, head = mine.shape
    samples = samples // CHUNKS
    rows = 2 * half
    return pl.pallas_call(
        functools.partial(forward_kernel, chunk * samples),
        out_shape=(
            kept_here(2, layers, samples, rows, head),
            kept_here(shards, samples, 2 * layers, rows, dtype=jnp.float32),
        ),
        in_specs=[SCALAR] * 3 + [FAST] * 3,
        out_specs=(FAST, FAST),
        compiler_params=ROOM,
    )(scalars, src_len, tgt_len, *held(mine, mate, kv))


def fetch(scalars, first, w_hbm, w_ref, w_sem):
    part = w_ref.shape[2]
    takes = []
    for k in range(w_ref.shape[0]):
        at = pl.ds(pl.multiple_of(scalars[4 + first + k] * part, part), part)
        takes.append(pltpu.make_async_copy(w_hbm.at[:, at], w_ref.at[k], w_sem.at[k]))
        takes[k].start()
    return takes


def fetched(count, weights):
    layers, width, cols = weights.shape
    return [pltpu.VMEM((count, layers, width // 4, cols), jnp.bfloat16), pltpu.SemaphoreType.DMA((count,))]


def terms_of(grads, weights):
    terms = None
    for r in range(grads.shape[0]):
        term = dot(grads[r], weights[r], NT)
        terms = term if terms is None else terms + term
    return low(terms)


def backward_kernel(start, keys, scalars, src_len, kv_ref, qc_ref, stat_ref, w_hbm,
                    keep_ref, give_ref, grads, up_ref, down_ref, w_ref, w_sem):
    (take,) = fetch(scalars, 0, w_hbm, w_ref, w_sem)
    layers, _, _ = kv_ref.shape
    _, _, samples, rows, head = qc_ref.shape
    shards = stat_ref.shape[0]
    scale = head ** (-0.5)
    seat = scalars[0]
    even = scalars[1] == 0

    def one(k, carry):
        b = start + k
        stat = stat_ref[:, k]
        lse = stat[:, :layers]
        top = jnp.max(lse, axis=0)
        weight = jnp.exp(lse - top[None])
        inverse = 1.0 / jnp.sum(weight, axis=0)
        delta = jnp.sum(weight * stat[:, layers:], axis=0) * inverse
        down_live = seat * keys + lax.broadcasted_iota(jnp.int32, (keys, rows), 0) < src_len[b]
        taken = pl.ds(pl.multiple_of(b * keys, keys), keys)
        at = pl.ds(pl.multiple_of(k * keys, keys), keys)
        for r in range(layers):
            pair = kv_ref[r, taken, :]
            key, value = pair[:, :head], pair[:, head:]
            query, grad = qc_ref[0, r, k], qc_ref[1, r, k]
            scores = jnp.where(down_live, dot(key, query, NT) * scale, masked_score)
            prob = jnp.exp(scores - top[r:r + 1, :]) * inverse[r:r + 1, :]
            slope = low(prob * (dot(value, grad, NT) - delta[r:r + 1, :]))
            prob = low(prob)
            grads[r, at, :head] = low(dot(slope, query, NN) * scale)
            grads[r, at, head:] = low(dot(prob, grad, NN))
            for kind, out in enumerate((dot(prob, value, TN), dot(slope, key, TN) * scale)):
                out = out.reshape(shards // 2, 2, rows // shards, head)
                keep_ref[:, kind, r, k] = low(jnp.where(even, out[:, 0], out[:, 1]))
                give_ref[:, kind, r, k] = low(jnp.where(even, out[:, 1], out[:, 0]))
        return carry

    lax.fori_loop(0, samples, one, 0)
    take.wait()
    terms = terms_of(grads, w_ref.at[0])
    half = up_ref.shape[0]
    up_ref[...] = terms[:half]
    down_ref[...] = terms[half:]


def backward(chunk, scalars, src_len, kv, qc, stats, weights):
    _, layers, samples, rows, head = qc.shape
    shards = stats.shape[0]
    half = kept_here(shards // 2, 2, layers, samples, rows // shards, head)
    count = kv.shape[1] // CHUNKS
    far = kept_here(count // 2, weights.shape[1] // 4)
    outs = (half, half, kept_here(layers, count, kv.shape[2]), far, far)
    return pl.pallas_call(
        functools.partial(backward_kernel, chunk * samples, count // samples),
        out_shape=outs,
        in_specs=[SCALAR] * 2 + [FAST] * 3 + [SLOW],
        out_specs=(FAST,) * len(outs),
        scratch_shapes=fetched(1, weights),
        compiler_params=ROOM,
    )(scalars, src_len, *held(kv, qc, stats), in_hbm(weights))


def near_kernel(scalars, grads, w_hbm, up_ref, down_ref, w_ref, w_sem):
    takes = fetch(scalars, 1, w_hbm, w_ref, w_sem)
    for side, ref in enumerate((up_ref, down_ref)):
        takes[side].wait()
        ref[...] = terms_of(grads, w_ref.at[side])


def near(scalars, grads, weights):
    outs = (kept_here(grads.shape[1], weights.shape[1] // 4),) * 2
    return pl.pallas_call(
        near_kernel,
        out_shape=outs,
        in_specs=[SCALAR, FAST, SLOW],
        out_specs=(FAST,) * len(outs),
        scratch_shapes=fetched(2, weights),
        compiler_params=ROOM,
    )(scalars, *held(grads), in_hbm(weights))


def here_kernel(scalars, grads, w_hbm, out_ref, w_ref, w_sem):
    (take,) = fetch(scalars, 3, w_hbm, w_ref, w_sem)
    take.wait()
    out_ref[...] = terms_of(grads, w_ref.at[0])


def here(scalars, grads, weights):
    return pl.pallas_call(
        here_kernel,
        out_shape=kept_here(grads.shape[1], weights.shape[1] // 4),
        in_specs=[SCALAR, FAST, SLOW],
        out_specs=FAST,
        scratch_shapes=fetched(1, weights),
        compiler_params=ROOM,
    )(scalars, *held(grads), in_hbm(weights))


def halve_kernel(parts, side, *refs):
    kept, came = refs[:parts], refs[parts:2 * parts]
    keep_ref, give_ref = refs[2 * parts:]
    count = keep_ref.shape[0]
    mine = pl.ds(side[0] * count, count)
    other = pl.ds((1 - side[0]) * count, count)
    size = keep_ref.shape[3] // parts
    for k in range(parts):
        at = slice(k * size, (k + 1) * size)
        keep_ref[:, :, :, at] = low(wide(kept[k][mine]) + wide(came[k][mine]))
        give_ref[:, :, :, at] = low(wide(kept[k][other]) + wide(came[k][other]))


def halve(side, kept, came):
    parts = len(kept)
    count, kinds, layers, samples, rows, head = kept[0].shape
    out = kept_here(count // 2, kinds, layers, samples * parts, rows, head)
    return pl.pallas_call(
        functools.partial(halve_kernel, parts),
        out_shape=(out, out),
        in_specs=[SCALAR] + [FAST] * (2 * parts),
        out_specs=(FAST, FAST),
        compiler_params=ROOM,
    )(side.reshape(1), *held(*kept, *came))


def deal_kernel(scalars, kept, came, *outs):
    for k, ref in enumerate(outs):
        layer = lax.rem(scalars[2] + k, len(outs))
        ref[...] = low(wide(kept[0, :, layer]) + wide(came[0, :, layer]))


def deal(scalars, kept, came):
    _, kinds, layers, samples, rows, head = kept.shape
    outs = (kept_here(kinds, samples, rows, head),) * layers
    return pl.pallas_call(
        deal_kernel, out_shape=outs, in_specs=[SCALAR, FAST, FAST], out_specs=(FAST,) * layers, compiler_params=ROOM, name="deal"
    )(scalars, *held(kept, came))


def pass_kernel(up_in, down_in, from_down, from_up, up_ref, down_ref):
    half = from_down.shape[0]
    up_ref[:half] = low(wide(up_in[:half]) + wide(from_down[...]))
    down_ref[half:] = low(wide(down_in[half:]) + wide(from_up[...]))
    up_ref[half:] = up_in[half:]
    down_ref[:half] = down_in[:half]


def pass_on(up_in, down_in, from_down, from_up):
    out = kept_here(*up_in.shape)
    return pl.pallas_call(
        pass_kernel, out_shape=(out, out), in_specs=[FAST] * 4, out_specs=(FAST, FAST), compiler_params=ROOM
    )(*held(up_in, down_in, from_down, from_up))


def gather_kernel(own, from_down, from_up, out_ref):
    heads, _, part = out_ref.shape
    for h in range(heads):
        at = slice(h * part, (h + 1) * part)
        out_ref[h] = low(wide(own[:, at]) + wide(from_down[:, at]) + wide(from_up[:, at]))


def gather(own, from_down, from_up, heads):
    count, width = from_down.shape
    return pl.pallas_call(
        gather_kernel,
        out_shape=kept_here(heads, count, width // heads),
        in_specs=[FAST] * 3,
        out_specs=FAST,
        compiler_params=ROOM,
    )(*held(own, from_down, from_up))


def finish_kernel(*refs):
    out_ref = refs[-1]
    count = out_ref.shape[0] // (len(refs) - 1)
    for c, ref in enumerate(refs[:-1]):
        total = wide(ref[0])
        for h in range(1, ref.shape[0]):
            total = total + wide(ref[h])
        out_ref[c * count:(c + 1) * count] = low(total)


def finish(pieces):
    _, count, part = pieces[0].shape
    return pl.pallas_call(
        finish_kernel,
        out_shape=bf(count * len(pieces), part),
        in_specs=[FAST] * len(pieces),
        out_specs=FAST,
        compiler_params=ROOM,
        name="finish",
    )(*held(*pieces))


def turn(count, by):
    return [(i, (i + by) % count) for i in range(count)]


def flip(count, bit):
    return [(i, i ^ bit) for i in range(count)]


def body(encoder_states, w_kv, queries, cotangent, src_len, tgt_len):
    sec = lax.axis_index("section")
    seat = lax.axis_index("seq")
    shards = lax.axis_size("seq")
    samples, src_rows, width = encoder_states.shape
    _, _, cols = w_kv.shape
    rows = queries.shape[2]
    half = rows // 2
    core = seat % 2
    places = [(sec + by) % 4 for by in (2, 1, 3, 0)]
    bits = [(seat // (1 << k)) % 2 for k in range(4)]
    scalars = jnp.stack([seat, core, sec, sec, *places, *bits]).astype(jnp.int32)

    def up(a):
        return lax.ppermute(a, "section", turn(4, 1))

    def down(a):
        return lax.ppermute(a, "section", turn(4, 3))

    def swap(a, axis):
        return lax.all_to_all(a, axis, 0, 0, tiled=True)

    halves = [
        jnp.transpose(lax.dynamic_slice_in_dim(a[0], core * half, half, 1), (2, 0, 1, 3)) for a in (queries, cotangent)
    ]
    mine = swap(jnp.stack(halves, 1), "section")
    kv = project(encoder_states.reshape(samples * src_rows, width), w_kv)
    mine, kv = lax.optimization_barrier((mine, kv))
    mate = lax.ppermute(mine, "seq", flip(shards, 1))
    heads = lax.axis_size("head")
    ready = []
    for c in range(CHUNKS):
        qc, stats = forward(c, shards, scalars, src_len, tgt_len, mine, mate, kv)
        ready.append((qc, swap(stats, "seq")))
    pieces, kept, came = [], [], []
    for c in range(CHUNKS):
        keep, give, grads, far_up, far_down = backward(c, scalars, src_len, kv, *ready[c], w_kv)
        came.append(lax.ppermute(give, "seq", flip(shards, 1)))
        kept.append(keep)
        far_up, far_down = up(far_up), down(far_down)
        to_up, to_down = near(scalars, grads, w_kv)
        own = here(scalars, grads, w_kv)
        to_up, to_down = pass_on(to_up, to_down, far_up, far_down)
        to_up, to_down = up(to_up), down(to_down)
        joined = gather(own, to_up, to_down, heads)
        pieces.append(swap(joined, "head"))
    source_grads = finish(pieces).reshape(samples, src_rows, cols)

    for bit in (3, 2, 1):
        keep, give = halve(bits[bit].astype(jnp.int32), kept, came)
        kept, came = [keep], [lax.ppermute(give, "seq", flip(shards, 1 << bit))]
    own, to_up, to_far, to_down = deal(scalars, kept[0], came[0])
    from_down, from_up = up(to_up), down(to_down)
    from_far = lax.ppermute(to_far, "section", turn(4, 2))
    ring = jnp.stack([own, from_down, from_far, from_up])
    groups = [lax.dynamic_index_in_dim(ring, (sec + 4 - g) % 4, 0, keepdims=False) for g in range(4)]
    od = jnp.stack(groups, axis=3)
    return od[0][None], od[1][None], source_grads


def solution(mesh):
    placed = (
        P(None, "seq", None),
        P(None, None, ("section", "head")),
        P("section", None, None, None, "head"),
        P("section", None, None, None, "head"),
        P(),
        P(),
    )

    return jax.shard_map(
        body,
        mesh=mesh,
        in_specs=placed,
        out_specs=(
            P("section", None, "seq", None, "head"),
            P("section", None, "seq", None, "head"),
            P(None, "seq", ("section", "head")),
        ),
        check_vma=False,
    )
```

```python
import functools

import jax
import jax.numpy as jnp
from jax import lax
from jax.experimental import pallas as pl
from jax.experimental.pallas import tpu as pltpu
from jax.sharding import PartitionSpec as P


masked_score = -1e30
NT = (((1,), (1,)), ((), ()))
NN = (((1,), (0,)), ((), ()))
TN = (((0,), (0,)), ((), ()))
CHUNKS = 2
GROUPED = (1, 3)


def dot(a, b, dims):
    return lax.dot_general(a, b, dims, preferred_element_type=jnp.float32)


def low(a):
    return a.astype(jnp.bfloat16)


def wide(a):
    return a.astype(jnp.float32)


def bf(*shape):
    return jax.ShapeDtypeStruct(shape, jnp.bfloat16)


def kept_here(*shape, dtype=jnp.bfloat16):
    return pltpu.VMEM(shape, dtype)


def held(*arrays):
    return [pltpu.with_memory_space_constraint(a, pltpu.VMEM) for a in arrays]


def in_hbm(array):
    return pltpu.with_memory_space_constraint(array, pltpu.HBM)


ROOM = pltpu.CompilerParams(vmem_limit_bytes=16 * 1024 * 1024)
FAST = pl.BlockSpec(memory_space=pltpu.VMEM)
SLOW = pl.BlockSpec(memory_space=pl.ANY)
SCALAR = pl.BlockSpec(memory_space=pltpu.SMEM)


def project_kernel(x_ref, w_ref, out_ref):
    out_ref[pl.program_id(0)] = low(dot(x_ref[...], w_ref[0], NN))


def project(rows, w_kv):
    layers, width, cols = w_kv.shape
    count = rows.shape[0]
    return pl.pallas_call(
        project_kernel,
        out_shape=kept_here(layers, count, cols),
        grid=(layers,),
        in_specs=[
            pl.BlockSpec((count, width), lambda r: (0, 0)),
            pl.BlockSpec((1, width, cols), lambda r: (r, 0, 0)),
        ],
        out_specs=FAST,
        compiler_params=ROOM,
        name="project",
    )(in_hbm(rows), in_hbm(w_kv))


def forward_kernel(scalars, src_len, tgt_len, mine, mate, kv_ref, qc_ref, stat_ref):
    seat, core = scalars[0], scalars[1]
    layers, count, _ = kv_ref.shape
    _, _, samples, rows, head = qc_ref.shape
    shards = stat_ref.shape[0]
    keys = count // samples
    scale = head ** (-0.5)
    first = core == 0

    def one(b, carry):
        live = lax.broadcasted_iota(jnp.int32, (rows, head), 0) < tgt_len[b]
        key_live = seat * keys + lax.broadcasted_iota(jnp.int32, (keys, rows), 0) < src_len[b]
        tops, deltas = [], []
        for r in range(layers):
            whole = []
            for kind in range(2):
                a, c = wide(mine[r, kind, b]), wide(mate[r, kind, b])
                whole.append(jnp.concatenate([jnp.where(first, a, c), jnp.where(first, c, a)], axis=0))
            query, grad = low(whole[0]), low(jnp.where(live, whole[1], 0.0))
            qc_ref[0, r, b] = query
            qc_ref[1, r, b] = grad
            pair = kv_ref[r, pl.ds(pl.multiple_of(b * keys, keys), keys), :]
            scores = jnp.where(key_live, dot(pair[:, :head], query, NT) * scale, masked_score)
            top = jnp.max(scores, axis=0, keepdims=True)
            power = jnp.exp(scores - top)
            total = jnp.sum(power, axis=0, keepdims=True)
            part = jnp.sum(power * dot(pair[:, head:], grad, NT), axis=0, keepdims=True)
            tops.append(top + jnp.log(total))
            deltas.append(part / total)
        stats = jnp.concatenate(tops + deltas, axis=0)
        for peer in range(shards):
            stat_ref[peer, b] = stats
        return carry

    lax.fori_loop(0, samples, one, 0)


def forward(shards, scalars, src_len, tgt_len, mine, mate, kv):
    layers, _, samples, half, head = mine.shape
    rows = 2 * half
    return pl.pallas_call(
        forward_kernel,
        out_shape=(
            kept_here(2, layers, samples, rows, head),
            kept_here(shards, samples, 2 * layers, rows, dtype=jnp.float32),
        ),
        in_specs=[SCALAR] * 3 + [FAST] * 3,
        out_specs=(FAST, FAST),
        compiler_params=ROOM,
        name="forward",
    )(scalars, src_len, tgt_len, *held(mine, mate, kv))


def terms_of(grads, w_ref, place):
    terms = None
    part = w_ref.shape[1] // 4
    at = pl.ds(pl.multiple_of(place * part, part), part)
    for r in range(grads.shape[0]):
        term = dot(grads[r], w_ref[r, at, :], NT)
        terms = term if terms is None else terms + term
    return low(terms)


def backward_kernel(start, keys, scalars, src_len, kv_ref, qc_ref, stat_ref, w_in,
                    keep_ref, give_ref, grads, up_ref, down_ref, *rest):
    layers, _, _ = kv_ref.shape
    rows, head = qc_ref.shape[3:]
    shards = stat_ref.shape[0]
    samples = keep_ref.shape[3]
    scale = head ** (-0.5)
    seat = scalars[0]
    even = scalars[1] == 0
    takes = []
    if rest:
        w_ref, w_sem = rest
        part = w_ref.shape[1] // 4
        for k in range(4):
            at = pl.ds(pl.multiple_of(scalars[4 + k] * part, part), part)
            takes.append(pltpu.make_async_copy(w_in.at[:, at], w_ref.at[:, at], w_sem.at[k]))
            takes[k].start()
    else:
        w_ref = w_in

    def one(k, carry):
        b = start + k
        stat = stat_ref[:, b]
        lse = stat[:, :layers]
        top = jnp.max(lse, axis=0)
        weight = jnp.exp(lse - top[None])
        inverse = 1.0 / jnp.sum(weight, axis=0)
        delta = jnp.sum(weight * stat[:, layers:], axis=0) * inverse
        down_live = seat * keys + lax.broadcasted_iota(jnp.int32, (keys, rows), 0) < src_len[b]
        taken = pl.ds(pl.multiple_of(b * keys, keys), keys)
        at = pl.ds(pl.multiple_of(k * keys, keys), keys)
        for r in range(layers):
            pair = kv_ref[r, taken, :]
            key, value = pair[:, :head], pair[:, head:]
            query, grad = qc_ref[0, r, b], qc_ref[1, r, b]
            scores = jnp.where(down_live, dot(key, query, NT) * scale, masked_score)
            prob = jnp.exp(scores - top[r:r + 1, :]) * inverse[r:r + 1, :]
            slope = low(prob * (dot(value, grad, NT) - delta[r:r + 1, :]))
            prob = low(prob)
            grads[r, at, :head] = low(dot(slope, query, NN) * scale)
            grads[r, at, head:] = low(dot(prob, grad, NN))
            for kind, out in enumerate((dot(prob, value, TN), dot(slope, key, TN) * scale)):
                out = out.reshape(shards // 2, 2, rows // shards, head)
                keep_ref[:, kind, r, k] = low(jnp.where(even, out[:, 0], out[:, 1]))
                give_ref[:, kind, r, k] = low(jnp.where(even, out[:, 1], out[:, 0]))
        return carry

    lax.fori_loop(0, samples, one, 0)
    for take in takes[:1]:
        take.wait()
    terms = terms_of(grads, w_ref, scalars[4])
    half = keys // 2
    for k in range(samples):
        up_ref[k * half:(k + 1) * half] = terms[k * keys:k * keys + half]
        down_ref[k * half:(k + 1) * half] = terms[k * keys + half:(k + 1) * keys]
    for take in takes[1:]:
        take.wait()


def backward(chunk, scalars, src_len, kv, qc, stats, weights):
    _, layers, samples, rows, head = qc.shape
    shards = stats.shape[0]
    keys = kv.shape[1] // samples
    samples = samples // CHUNKS
    half = kept_here(shards // 2, 2, layers, samples, rows // shards, head)
    far = kept_here(samples * keys // 2, weights.shape[1] // 4)
    outs = (half, half, kept_here(layers, samples * keys, kv.shape[2]), far, far)
    scratch = []
    if chunk == 0:
        outs += (kept_here(*weights.shape),)
        scratch = [pltpu.SemaphoreType.DMA((4,))]
        weights = in_hbm(weights)
    else:
        (weights,) = held(weights)
    return pl.pallas_call(
        functools.partial(backward_kernel, chunk * samples, keys),
        out_shape=outs,
        in_specs=[SCALAR] * 2 + [FAST] * 3 + [FAST if chunk else SLOW],
        out_specs=(FAST,) * len(outs),
        scratch_shapes=scratch,
        compiler_params=ROOM,
    )(scalars, src_len, *held(kv, qc, stats), weights)


def near_kernel(scalars, *refs):
    grads, w_ref, outs = refs[:CHUNKS], refs[CHUNKS], refs[CHUNKS + 1:]
    groups = len(outs) // 2
    for side in range(2):
        done = 0
        terms = [terms_of(g, w_ref, scalars[5 + side]) for g in grads]
        size = terms[0].shape[0]
        for k in range(groups):
            ref = outs[side * groups + k]
            filled = 0
            while filled < ref.shape[0]:
                chunk, at = divmod(done + filled, size)
                count = min(ref.shape[0] - filled, size - at)
                ref[filled:filled + count] = terms[chunk][at:at + count]
                filled += count
            done += filled


def near(scalars, grads, weights, keys):
    outs = tuple(kept_here(g * keys, weights.shape[1] // 4) for g in GROUPED) * 2
    return pl.pallas_call(
        near_kernel,
        out_shape=outs,
        in_specs=[SCALAR] + [FAST] * (len(grads) + 1),
        out_specs=(FAST,) * len(outs),
        compiler_params=ROOM,
        name="near",
    )(scalars, *held(*grads, weights))


def here_kernel(scalars, *refs):
    grads, w_ref, out_ref = refs[:-2], refs[-2], refs[-1]
    size = grads[0].shape[1]
    for k, part in enumerate(grads):
        out_ref[k * size:(k + 1) * size] = terms_of(part, w_ref, scalars[7])


def here(scalars, grads, weights):
    count = sum(g.shape[1] for g in grads)
    return pl.pallas_call(
        here_kernel,
        out_shape=kept_here(count, weights.shape[1] // 4),
        in_specs=[SCALAR] + [FAST] * (len(grads) + 1),
        out_specs=FAST,
        compiler_params=ROOM,
        name="here",
    )(scalars, *held(*grads, weights))


def halve_kernel(parts, run, side, *refs):
    kept, came = refs[:parts], refs[parts:2 * parts]
    keep_ref, give_ref = refs[2 * parts:]
    size = keep_ref.shape[3] // parts
    for start in range(0, keep_ref.shape[0], run):
        mine = pl.ds(2 * start + side[0] * run, run)
        other = pl.ds(2 * start + (1 - side[0]) * run, run)
        to = slice(start, start + run)
        for k in range(parts):
            at = slice(k * size, (k + 1) * size)
            keep_ref[to, :, :, at] = low(wide(kept[k][mine]) + wide(came[k][mine]))
            give_ref[to, :, :, at] = low(wide(kept[k][other]) + wide(came[k][other]))


def halve(side, kept, came, run):
    parts = len(kept)
    count, kinds, layers, samples, rows, head = kept[0].shape
    out = kept_here(count // 2, kinds, layers, samples * parts, rows, head)
    return pl.pallas_call(
        functools.partial(halve_kernel, parts, run),
        out_shape=(out, out),
        in_specs=[SCALAR] + [FAST] * (2 * parts),
        out_specs=(FAST, FAST),
        compiler_params=ROOM,
    )(side.reshape(1), *held(*kept, *came))


def deal_kernel(scalars, kept, came, *outs):
    for k, ref in enumerate(outs):
        layer = lax.rem(scalars[2] + k, len(outs))
        ref[...] = low(wide(kept[0, :, layer]) + wide(came[0, :, layer]))


def deal(scalars, kept, came):
    _, kinds, layers, samples, rows, head = kept.shape
    outs = (kept_here(kinds, samples, rows, head),) * layers
    return pl.pallas_call(
        deal_kernel, out_shape=outs, in_specs=[SCALAR, FAST, FAST], out_specs=(FAST,) * layers, compiler_params=ROOM, name="deal"
    )(scalars, *held(kept, came))


def pass_kernel(keys, start, up_in, down_in, *refs):
    ups, downs = refs[:(len(refs) - 2) // 2], refs[(len(refs) - 2) // 2:-2]
    up_ref, down_ref = refs[-2:]
    half = keys // 2
    per = ups[0].shape[0] // half
    first = start // per
    for k in range(up_in.shape[0] // keys):
        chunk, place = divmod(start + k, per)
        came = slice(place * half, (place + 1) * half)
        top, bottom = slice(k * keys, k * keys + half), slice(k * keys + half, (k + 1) * keys)
        up_ref[top] = low(wide(up_in[top]) + wide(ups[chunk - first][came]))
        down_ref[bottom] = low(wide(down_in[bottom]) + wide(downs[chunk - first][came]))
        up_ref[bottom] = up_in[bottom]
        down_ref[top] = down_in[top]


def pass_on(keys, start, up_in, down_in, ups, downs):
    per = ups[0].shape[0] // (keys // 2)
    last = (start + up_in.shape[0] // keys - 1) // per
    ups, downs = ups[start // per:last + 1], downs[start // per:last + 1]
    out = kept_here(*up_in.shape)
    return pl.pallas_call(
        functools.partial(pass_kernel, keys, start),
        out_shape=(out, out),
        in_specs=[FAST] * (2 + 2 * len(ups)),
        out_specs=(FAST, FAST),
        compiler_params=ROOM,
    )(*held(up_in, down_in, *ups, *downs))


def gather_kernel(start, own, from_down, from_up, out_ref):
    heads, count, part = out_ref.shape
    for h in range(heads):
        at = slice(h * part, (h + 1) * part)
        out_ref[h] = low(wide(own[start:start + count, at]) + wide(from_down[:, at]) + wide(from_up[:, at]))


def gather(start, own, from_down, from_up, heads):
    count, width = from_down.shape
    return pl.pallas_call(
        functools.partial(gather_kernel, start),
        out_shape=kept_here(heads, count, width // heads),
        in_specs=[FAST] * 3,
        out_specs=FAST,
        compiler_params=ROOM,
    )(*held(own, from_down, from_up))


def finish_kernel(*refs):
    out_ref = refs[-1]
    start = 0
    for ref in refs[:-1]:
        total = wide(ref[0])
        for h in range(1, ref.shape[0]):
            total = total + wide(ref[h])
        out_ref[start:start + ref.shape[1]] = low(total)
        start += ref.shape[1]


def finish(pieces):
    return pl.pallas_call(
        finish_kernel,
        out_shape=bf(sum(p.shape[1] for p in pieces), pieces[0].shape[2]),
        in_specs=[FAST] * len(pieces),
        out_specs=FAST,
        compiler_params=ROOM,
        name="finish",
    )(*held(*pieces))


def turn(count, by):
    return [(i, (i + by) % count) for i in range(count)]


def flip(count, bit):
    return [(i, i ^ bit) for i in range(count)]


def body(encoder_states, w_kv, queries, cotangent, src_len, tgt_len):
    sec = lax.axis_index("section")
    seat = lax.axis_index("seq")
    shards = lax.axis_size("seq")
    samples, src_rows, width = encoder_states.shape
    _, _, cols = w_kv.shape
    rows = queries.shape[2]
    half = rows // 2
    core = seat % 2
    places = [(sec + by) % 4 for by in (2, 1, 3, 0)]
    bits = [(seat // (1 << k)) % 2 for k in range(4)]
    scalars = jnp.stack([seat, core, sec, sec, *places, *bits]).astype(jnp.int32)

    def up(a):
        return lax.ppermute(a, "section", turn(4, 1))

    def down(a):
        return lax.ppermute(a, "section", turn(4, 3))

    def swap(a, axis):
        return lax.all_to_all(a, axis, 0, 0, tiled=True)

    halves = [
        jnp.transpose(lax.dynamic_slice_in_dim(a[0], core * half, half, 1), (2, 0, 1, 3)) for a in (queries, cotangent)
    ]
    mine = swap(jnp.stack(halves, 1), "section")
    kv = project(encoder_states.reshape(samples * src_rows, width), w_kv)
    mine, kv = lax.optimization_barrier((mine, kv))
    mate = lax.ppermute(mine, "seq", flip(shards, 1))
    qc, stats = forward(shards, scalars, src_len, tgt_len, mine, mate, kv)
    stats = swap(stats, "seq")

    heads = lax.axis_size("head")
    weights = w_kv
    kept, came, grads, ups, downs = [], [], [], [], []
    for c in range(CHUNKS):
        keep, give, part, far_up, far_down, *copied = backward(c, scalars, src_len, kv, qc, stats, weights)
        weights = copied[0] if copied else weights
        ups.append(up(far_up))
        downs.append(down(far_down))
        came.append(lax.ppermute(give, "seq", flip(shards, 1)))
        kept.append(keep)
        grads.append(part)
    sides = near(scalars, grads, weights, src_rows)
    own = here(scalars, grads, weights)
    pieces = []
    start = 0
    for c, group in enumerate(GROUPED):
        to_up, to_down = pass_on(src_rows, start, sides[c], sides[len(GROUPED) + c], ups, downs)
        to_up, to_down = up(to_up), down(to_down)
        joined = gather(start * src_rows, own, to_up, to_down, heads)
        pieces.append(swap(joined, "head"))
        start += group
    source_grads = finish(pieces).reshape(samples, src_rows, cols)

    for bit, run in ((1, 1), (3, 2), (2, 1)):
        keep, give = halve(bits[bit].astype(jnp.int32), kept, came, run)
        kept, came = [keep], [lax.ppermute(give, "seq", flip(shards, 1 << bit))]
    own, to_up, to_far, to_down = deal(scalars, kept[0], came[0])
    from_down, from_up = up(to_up), down(to_down)
    from_far = lax.ppermute(to_far, "section", turn(4, 2))
    ring = jnp.stack([own, from_down, from_far, from_up])
    groups = [lax.dynamic_index_in_dim(ring, (sec + 4 - g) % 4, 0, keepdims=False) for g in range(4)]
    od = jnp.stack(groups, axis=3)
    return od[0][None], od[1][None], source_grads


def solution(mesh):
    placed = (
        P(None, "seq", None),
        P(None, None, ("section", "head")),
        P("section", None, None, None, "head"),
        P("section", None, None, None, "head"),
        P(),
        P(),
    )

    return jax.shard_map(
        body,
        mesh=mesh,
        in_specs=placed,
        out_specs=(
            P("section", None, "seq", None, "head"),
            P("section", None, "seq", None, "head"),
            P(None, "seq", ("section", "head")),
        ),
        check_vma=False,
    )
```

```python
import functools

import jax
import jax.numpy as jnp
from jax import lax
from jax.experimental import pallas as pl
from jax.experimental.pallas import tpu as pltpu
from jax.sharding import PartitionSpec as P


masked_score = -1e30
NT = (((1,), (1,)), ((), ()))
NN = (((1,), (0,)), ((), ()))
TN = (((0,), (0,)), ((), ()))
CHUNKS = 2
GROUPED = (1, 3)


def dot(a, b, dims):
    return lax.dot_general(a, b, dims, preferred_element_type=jnp.float32)


def low(a):
    return a.astype(jnp.bfloat16)


def wide(a):
    return a.astype(jnp.float32)


def bf(*shape):
    return jax.ShapeDtypeStruct(shape, jnp.bfloat16)


def kept_here(*shape, dtype=jnp.bfloat16):
    return pltpu.VMEM(shape, dtype)


def held(*arrays):
    return [pltpu.with_memory_space_constraint(a, pltpu.VMEM) for a in arrays]


def in_hbm(array):
    return pltpu.with_memory_space_constraint(array, pltpu.HBM)


ROOM = pltpu.CompilerParams(vmem_limit_bytes=16 * 1024 * 1024)
FAST = pl.BlockSpec(memory_space=pltpu.VMEM)
SLOW = pl.BlockSpec(memory_space=pl.ANY)
SCALAR = pl.BlockSpec(memory_space=pltpu.SMEM)


def project_kernel(x_ref, w_ref, out_ref):
    out_ref[pl.program_id(0)] = low(dot(x_ref[...], w_ref[0], NN))


def project(rows, w_kv):
    layers, width, cols = w_kv.shape
    count = rows.shape[0]
    return pl.pallas_call(
        project_kernel,
        out_shape=kept_here(layers, count, cols),
        grid=(layers,),
        in_specs=[
            pl.BlockSpec((count, width), lambda r: (0, 0)),
            pl.BlockSpec((1, width, cols), lambda r: (r, 0, 0)),
        ],
        out_specs=FAST,
        compiler_params=ROOM,
        name="project",
    )(in_hbm(rows), in_hbm(w_kv))


def key_places(seat, keys, targets):
    at = lax.broadcasted_iota(jnp.int32, (2 * keys, targets), 0)
    other = seat + 1 - 2 * lax.rem(seat, 2)
    return at + jnp.where(at < keys, seat * keys, other * keys - keys)


def live_targets(core, targets, block, head, limit):
    at = lax.broadcasted_iota(jnp.int32, (targets, head), 0)
    return (at // block) * (2 * block) + core * block + lax.rem(at, block) < limit


def forward_kernel(block, scalars, src_len, tgt_len, mine, kv_ref, mate_ref, stat_ref):
    seat, core = scalars[0], scalars[1]
    layers, count, _ = kv_ref.shape
    _, _, samples, rows, head = mine.shape
    keys = count // samples
    scale = head ** (-0.5)

    def one(b, carry):
        live = live_targets(core, rows, block, head, tgt_len[b])
        key_live = key_places(seat, keys, rows) < src_len[b]
        at = pl.ds(pl.multiple_of(b * keys, keys), keys)
        tops, deltas = [], []
        for r in range(layers):
            query = mine[r, 0, b]
            grad = low(jnp.where(live, wide(mine[r, 1, b]), 0.0))
            pair = jnp.concatenate([kv_ref[r, at, :], mate_ref[r, at, :]], axis=0)
            scores = jnp.where(key_live, dot(pair[:, :head], query, NT) * scale, masked_score)
            top = jnp.max(scores, axis=0, keepdims=True)
            power = jnp.exp(scores - top)
            total = jnp.sum(power, axis=0, keepdims=True)
            part = jnp.sum(power * dot(pair[:, head:], grad, NT), axis=0, keepdims=True)
            tops.append(top + jnp.log(total))
            deltas.append(part / total)
        stats = jnp.concatenate(tops + deltas, axis=0)
        for peer in range(stat_ref.shape[0]):
            stat_ref[peer, b] = stats
        return carry

    lax.fori_loop(0, samples, one, 0)


def forward(chips, block, scalars, src_len, tgt_len, mine, kv, mate):
    layers, _, samples, rows, _ = mine.shape
    return pl.pallas_call(
        functools.partial(forward_kernel, block),
        out_shape=kept_here(chips, samples, 2 * layers, rows, dtype=jnp.float32),
        in_specs=[SCALAR] * 3 + [FAST] * 3,
        out_specs=FAST,
        compiler_params=ROOM,
        name="forward",
    )(scalars, src_len, tgt_len, *held(mine, kv, mate))


def terms_of(grads, w_ref, place):
    terms = None
    part = w_ref.shape[1] // 4
    at = pl.ds(pl.multiple_of(place * part, part), part)
    for r in range(grads.shape[0]):
        term = dot(grads[r], w_ref[r, at, :], NT)
        terms = term if terms is None else terms + term
    return low(terms)


def backward_kernel(start, keys, scalars, src_len, tgt_len, mine, kv_ref, mate_ref, stat_ref, w_hbm,
                    keep_ref, give_ref, grads_ref, mate_grads_ref, *rest):
    layers, _, _ = kv_ref.shape
    rows, head = mine.shape[3:]
    half, _, _, samples, block, _ = keep_ref.shape
    scale = head ** (-0.5)
    seat, core = scalars[0], scalars[1]
    even = scalars[9] == 0
    takes = []
    if rest:
        w_ref, w_sem = rest
        take = pltpu.make_async_copy(w_hbm, w_ref, w_sem)
        take.start()
        takes.append(take)

    def one(k, carry):
        b = start + k
        stat = stat_ref[:, b]
        lse = stat[:, :layers]
        top = jnp.max(lse, axis=0)
        weight = jnp.exp(lse - top[None])
        inverse = 1.0 / jnp.sum(weight, axis=0)
        delta = jnp.sum(weight * stat[:, layers:], axis=0) * inverse
        live = live_targets(core, rows, block, head, tgt_len[b])
        key_live = key_places(seat, keys, rows) < src_len[b]
        taken = pl.ds(pl.multiple_of(b * keys, keys), keys)
        at = pl.ds(pl.multiple_of(k * keys, keys), keys)
        for r in range(layers):
            pair = jnp.concatenate([kv_ref[r, taken, :], mate_ref[r, taken, :]], axis=0)
            key, value = pair[:, :head], pair[:, head:]
            query = mine[r, 0, b]
            grad = low(jnp.where(live, wide(mine[r, 1, b]), 0.0))
            scores = jnp.where(key_live, dot(key, query, NT) * scale, masked_score)
            prob = jnp.exp(scores - top[r:r + 1, :]) * inverse[r:r + 1, :]
            slope = low(prob * (dot(value, grad, NT) - delta[r:r + 1, :]))
            prob = low(prob)
            both = (low(dot(slope, query, NN) * scale), low(dot(prob, grad, NN)))
            for side in range(2):
                columns = slice(side * head, (side + 1) * head)
                grads_ref[r, at, columns] = both[side][:keys]
                mate_grads_ref[r, at, columns] = both[side][keys:]
            for kind, out in enumerate((dot(prob, value, TN), dot(slope, key, TN) * scale)):
                out = out.reshape(half, 2, block, head)
                keep_ref[:, kind, r, k] = low(jnp.where(even, out[:, 0], out[:, 1]))
                give_ref[:, kind, r, k] = low(jnp.where(even, out[:, 1], out[:, 0]))
        return carry

    lax.fori_loop(0, samples, one, 0)
    for take in takes:
        take.wait()


def backward(chunk, block, scalars, src_len, tgt_len, mine, kv, mate, stats, weights):
    layers, _, samples, rows, head = mine.shape
    keys = kv.shape[1] // samples
    samples = samples // CHUNKS
    half = kept_here(rows // block // 2, 2, layers, samples, block, head)
    grads = kept_here(layers, samples * keys, kv.shape[2])
    outs = (half, half, grads, grads)
    scratch = []
    if chunk == 0:
        outs += (kept_here(*weights.shape),)
        scratch = [pltpu.SemaphoreType.DMA]
    return pl.pallas_call(
        functools.partial(backward_kernel, chunk * samples, keys),
        out_shape=outs,
        in_specs=[SCALAR] * 3 + [FAST] * 4 + [SLOW],
        out_specs=(FAST,) * len(outs),
        scratch_shapes=scratch,
        compiler_params=ROOM,
    )(scalars, src_len, tgt_len, *held(mine, kv, mate, stats), in_hbm(weights))


def join_kernel(keys, scalars, grads_in, came, w_ref, grads, up_ref, down_ref):
    grads[...] = low(wide(grads_in[...]) + wide(came[...]))
    terms = terms_of(grads, w_ref, scalars[4])
    half = keys // 2
    for k in range(grads.shape[1] // keys):
        up_ref[k * half:(k + 1) * half] = terms[k * keys:k * keys + half]
        down_ref[k * half:(k + 1) * half] = terms[k * keys + half:(k + 1) * keys]


def join(keys, scalars, grads, came, weights):
    far = kept_here(grads.shape[1] // 2, weights.shape[1] // 4)
    outs = (kept_here(*grads.shape), far, far)
    return pl.pallas_call(
        functools.partial(join_kernel, keys),
        out_shape=outs,
        in_specs=[SCALAR] + [FAST] * 3,
        out_specs=(FAST,) * 3,
        compiler_params=ROOM,
    )(scalars, *held(grads, came, weights))


def near_kernel(scalars, *refs):
    grads, w_ref, outs = refs[:CHUNKS], refs[CHUNKS], refs[CHUNKS + 1:]
    groups = len(outs) // 2
    for side in range(2):
        done = 0
        terms = [terms_of(g, w_ref, scalars[5 + side]) for g in grads]
        size = terms[0].shape[0]
        for k in range(groups):
            ref = outs[side * groups + k]
            filled = 0
            while filled < ref.shape[0]:
                chunk, at = divmod(done + filled, size)
                count = min(ref.shape[0] - filled, size - at)
                ref[filled:filled + count] = terms[chunk][at:at + count]
                filled += count
            done += filled


def near(scalars, grads, weights, keys):
    outs = tuple(kept_here(g * keys, weights.shape[1] // 4) for g in GROUPED) * 2
    return pl.pallas_call(
        near_kernel,
        out_shape=outs,
        in_specs=[SCALAR] + [FAST] * (len(grads) + 1),
        out_specs=(FAST,) * len(outs),
        compiler_params=ROOM,
        name="near",
    )(scalars, *held(*grads, weights))


def here_kernel(scalars, *refs):
    grads, w_ref, out_ref = refs[:-2], refs[-2], refs[-1]
    size = grads[0].shape[1]
    for k, part in enumerate(grads):
        out_ref[k * size:(k + 1) * size] = terms_of(part, w_ref, scalars[7])


def here(scalars, grads, weights):
    count = sum(g.shape[1] for g in grads)
    return pl.pallas_call(
        here_kernel,
        out_shape=kept_here(count, weights.shape[1] // 4),
        in_specs=[SCALAR] + [FAST] * (len(grads) + 1),
        out_specs=FAST,
        compiler_params=ROOM,
        name="here",
    )(scalars, *held(*grads, weights))


def halve_kernel(parts, run, side, *refs):
    kept, came = refs[:parts], refs[parts:2 * parts]
    keep_ref, give_ref = refs[2 * parts:]
    size = keep_ref.shape[3] // parts
    for start in range(0, keep_ref.shape[0], run):
        mine = pl.ds(2 * start + side[0] * run, run)
        other = pl.ds(2 * start + (1 - side[0]) * run, run)
        to = slice(start, start + run)
        for k in range(parts):
            at = slice(k * size, (k + 1) * size)
            keep_ref[to, :, :, at] = low(wide(kept[k][mine]) + wide(came[k][mine]))
            give_ref[to, :, :, at] = low(wide(kept[k][other]) + wide(came[k][other]))


def halve(side, kept, came, run):
    parts = len(kept)
    count, kinds, layers, samples, rows, head = kept[0].shape
    out = kept_here(count // 2, kinds, layers, samples * parts, rows, head)
    return pl.pallas_call(
        functools.partial(halve_kernel, parts, run),
        out_shape=(out, out),
        in_specs=[SCALAR] + [FAST] * (2 * parts),
        out_specs=(FAST, FAST),
        compiler_params=ROOM,
    )(side.reshape(1), *held(*kept, *came))


def deal_kernel(scalars, kept, came, *outs):
    for k, ref in enumerate(outs):
        layer = lax.rem(scalars[2] + k, len(outs))
        ref[...] = low(wide(kept[0, :, layer]) + wide(came[0, :, layer]))


def deal(scalars, kept, came):
    _, kinds, layers, samples, rows, head = kept.shape
    outs = (kept_here(kinds, samples, rows, head),) * layers
    return pl.pallas_call(
        deal_kernel, out_shape=outs, in_specs=[SCALAR, FAST, FAST], out_specs=(FAST,) * layers, compiler_params=ROOM, name="deal"
    )(scalars, *held(kept, came))


def pass_kernel(keys, start, up_in, down_in, *refs):
    ups, downs = refs[:(len(refs) - 2) // 2], refs[(len(refs) - 2) // 2:-2]
    up_ref, down_ref = refs[-2:]
    half = keys // 2
    per = ups[0].shape[0] // half
    first = start // per
    for k in range(up_in.shape[0] // keys):
        chunk, place = divmod(start + k, per)
        came = slice(place * half, (place + 1) * half)
        top, bottom = slice(k * keys, k * keys + half), slice(k * keys + half, (k + 1) * keys)
        up_ref[top] = low(wide(up_in[top]) + wide(ups[chunk - first][came]))
        down_ref[bottom] = low(wide(down_in[bottom]) + wide(downs[chunk - first][came]))
        up_ref[bottom] = up_in[bottom]
        down_ref[top] = down_in[top]


def pass_on(keys, start, up_in, down_in, ups, downs):
    per = ups[0].shape[0] // (keys // 2)
    last = (start + up_in.shape[0] // keys - 1) // per
    ups, downs = ups[start // per:last + 1], downs[start // per:last + 1]
    out = kept_here(*up_in.shape)
    return pl.pallas_call(
        functools.partial(pass_kernel, keys, start),
        out_shape=(out, out),
        in_specs=[FAST] * (2 + 2 * len(ups)),
        out_specs=(FAST, FAST),
        compiler_params=ROOM,
    )(*held(up_in, down_in, *ups, *downs))


def gather_kernel(start, own, from_down, from_up, out_ref):
    heads, count, part = out_ref.shape
    for h in range(heads):
        at = slice(h * part, (h + 1) * part)
        out_ref[h] = low(wide(own[start:start + count, at]) + wide(from_down[:, at]) + wide(from_up[:, at]))


def gather(start, own, from_down, from_up, heads):
    count, width = from_down.shape
    return pl.pallas_call(
        functools.partial(gather_kernel, start),
        out_shape=kept_here(heads, count, width // heads),
        in_specs=[FAST] * 3,
        out_specs=FAST,
        compiler_params=ROOM,
    )(*held(own, from_down, from_up))


def finish_kernel(*refs):
    out_ref = refs[-1]
    start = 0
    for ref in refs[:-1]:
        total = wide(ref[0])
        for h in range(1, ref.shape[0]):
            total = total + wide(ref[h])
        out_ref[start:start + ref.shape[1]] = low(total)
        start += ref.shape[1]


def finish(pieces):
    return pl.pallas_call(
        finish_kernel,
        out_shape=bf(sum(p.shape[1] for p in pieces), pieces[0].shape[2]),
        in_specs=[FAST] * len(pieces),
        out_specs=FAST,
        compiler_params=ROOM,
        name="finish",
    )(*held(*pieces))


def turn(count, by):
    return [(i, (i + by) % count) for i in range(count)]


def flip(count, bit):
    return [(i, i ^ bit) for i in range(count)]


def body(encoder_states, w_kv, queries, cotangent, src_len, tgt_len):
    sec = lax.axis_index("section")
    seat = lax.axis_index("seq")
    shards = lax.axis_size("seq")
    samples, src_rows, width = encoder_states.shape
    _, _, cols = w_kv.shape
    rows = queries.shape[2]
    half = rows // 2
    core = seat % 2
    places = [(sec + by) % 4 for by in (2, 1, 3, 0)]
    bits = [(seat // (1 << k)) % 2 for k in range(4)]
    scalars = jnp.stack([seat, core, sec, sec, *places, *bits]).astype(jnp.int32)

    def up(a):
        return lax.ppermute(a, "section", turn(4, 1))

    def down(a):
        return lax.ppermute(a, "section", turn(4, 3))

    def swap(a, axis):
        return lax.all_to_all(a, axis, 0, 0, tiled=True)

    block = rows // shards
    halves = []
    for source in (queries, cotangent):
        picked = source[0].reshape(samples, shards // 2, 2, block, *source.shape[3:])
        picked = lax.dynamic_index_in_dim(picked, core, 2, keepdims=False)
        picked = picked.reshape(samples, half, *source.shape[3:])
        halves.append(jnp.transpose(picked, (2, 0, 1, 3)))
    mine = swap(jnp.stack(halves, 1), "section")
    kv = project(encoder_states.reshape(samples * src_rows, width), w_kv)
    mate = lax.ppermute(kv, "seq", flip(shards, 1))
    mine, kv = lax.optimization_barrier((mine, kv))
    stats = forward(shards // 2, block, scalars, src_len, tgt_len, mine, kv, mate)
    same_core = [list(range(c, shards, 2)) for c in range(2)]
    stats = lax.all_to_all(stats, "seq", 0, 0, axis_index_groups=same_core, tiled=True)

    heads = lax.axis_size("head")
    kept, came, parts, grads, ups, downs = [], [], [], [], [], []
    weights = w_kv
    for c in range(CHUNKS):
        keep, give, own, other, *copied = backward(
            c, block, scalars, src_len, tgt_len, mine, kv, mate, stats, w_kv
        )
        weights = copied[0] if copied else weights
        parts.append((own, lax.ppermute(other, "seq", flip(shards, 1))))
        came.append(lax.ppermute(give, "seq", flip(shards, 2)))
        kept.append(keep)
    for c in range(CHUNKS):
        part, far_up, far_down = join(src_rows, scalars, *parts[c], weights)
        ups.append(up(far_up))
        downs.append(down(far_down))
        grads.append(part)
    sides = near(scalars, grads, weights, src_rows)
    own = here(scalars, grads, weights)
    pieces = []
    start = 0
    for c, group in enumerate(GROUPED):
        to_up, to_down = pass_on(src_rows, start, sides[c], sides[len(GROUPED) + c], ups, downs)
        to_up, to_down = up(to_up), down(to_down)
        joined = gather(start * src_rows, own, to_up, to_down, heads)
        pieces.append(swap(joined, "head"))
        start += group
    source_grads = finish(pieces).reshape(samples, src_rows, cols)

    for bit, run in ((3, 2), (2, 1)):
        keep, give = halve(bits[bit].astype(jnp.int32), kept, came, run)
        kept, came = [keep], [lax.ppermute(give, "seq", flip(shards, 1 << bit))]
    own, to_up, to_far, to_down = deal(scalars, kept[0], came[0])
    from_down, from_up = up(to_up), down(to_down)
    from_far = lax.ppermute(to_far, "section", turn(4, 2))
    ring = jnp.stack([own, from_down, from_far, from_up])
    groups = [lax.dynamic_index_in_dim(ring, (sec + 4 - g) % 4, 0, keepdims=False) for g in range(4)]
    od = jnp.stack(groups, axis=3)
    return od[0][None], od[1][None], source_grads


def solution(mesh):
    placed = (
        P(None, "seq", None),
        P(None, None, ("section", "head")),
        P("section", None, None, None, "head"),
        P("section", None, None, None, "head"),
        P(),
        P(),
    )

    return jax.shard_map(
        body,
        mesh=mesh,
        in_specs=placed,
        out_specs=(
            P("section", None, "seq", None, "head"),
            P("section", None, "seq", None, "head"),
            P(None, "seq", ("section", "head")),
        ),
        check_vma=False,
    )
```

```python
import functools

import jax
import jax.numpy as jnp
from jax import lax
from jax.experimental import pallas as pl
from jax.experimental.pallas import tpu as pltpu
from jax.sharding import PartitionSpec as P


masked_score = -1e30
NT = (((1,), (1,)), ((), ()))
NN = (((1,), (0,)), ((), ()))
TN = (((0,), (0,)), ((), ()))
CHUNKS = 2
LEAVING = 3


def dot(a, b, dims):
    return lax.dot_general(a, b, dims, preferred_element_type=jnp.float32)


def low(a):
    return a.astype(jnp.bfloat16)


def wide(a):
    return a.astype(jnp.float32)


def bf(*shape):
    return jax.ShapeDtypeStruct(shape, jnp.bfloat16)


def kept_here(*shape, dtype=jnp.bfloat16):
    return pltpu.VMEM(shape, dtype)


def held(*arrays):
    return [pltpu.with_memory_space_constraint(a, pltpu.VMEM) for a in arrays]


def in_hbm(array):
    return pltpu.with_memory_space_constraint(array, pltpu.HBM)


ROOM = pltpu.CompilerParams(vmem_limit_bytes=16 * 1024 * 1024)
FAST = pl.BlockSpec(memory_space=pltpu.VMEM)
SLOW = pl.BlockSpec(memory_space=pl.ANY)
SCALAR = pl.BlockSpec(memory_space=pltpu.SMEM)


def project_kernel(x_ref, w_ref, out_ref):
    out_ref[pl.program_id(0)] = low(dot(x_ref[...], w_ref[0], NN))


def project(rows, w_kv):
    layers, width, cols = w_kv.shape
    count = rows.shape[0]
    return pl.pallas_call(
        project_kernel,
        out_shape=kept_here(layers, count, cols),
        grid=(layers,),
        in_specs=[
            pl.BlockSpec((count, width), lambda r: (0, 0)),
            pl.BlockSpec((1, width, cols), lambda r: (r, 0, 0)),
        ],
        out_specs=FAST,
        compiler_params=ROOM,
        name="project",
    )(in_hbm(rows), in_hbm(w_kv))


def key_places(seat, keys, targets):
    at = lax.broadcasted_iota(jnp.int32, (2 * keys, targets), 0)
    other = seat + 1 - 2 * lax.rem(seat, 2)
    return at + jnp.where(at < keys, seat * keys, other * keys - keys)


def live_targets(core, targets, block, head, limit):
    at = lax.broadcasted_iota(jnp.int32, (targets, head), 0)
    return (at // block) * (2 * block) + core * block + lax.rem(at, block) < limit


def forward_kernel(block, scalars, src_len, tgt_len, mine, kv_ref, mate_ref, stat_ref):
    seat, core = scalars[0], scalars[1]
    layers, count, _ = kv_ref.shape
    _, _, samples, rows, head = mine.shape
    keys = count // samples
    scale = head ** (-0.5)

    def one(b, carry):
        live = live_targets(core, rows, block, head, tgt_len[b])
        key_live = key_places(seat, keys, rows) < src_len[b]
        at = pl.ds(pl.multiple_of(b * keys, keys), keys)
        tops, deltas = [], []
        for r in range(layers):
            query = mine[r, 0, b]
            grad = low(jnp.where(live, wide(mine[r, 1, b]), 0.0))
            pair = jnp.concatenate([kv_ref[r, at, :], mate_ref[r, at, :]], axis=0)
            scores = jnp.where(key_live, dot(pair[:, :head], query, NT) * scale, masked_score)
            top = jnp.max(scores, axis=0, keepdims=True)
            power = jnp.exp(scores - top)
            total = jnp.sum(power, axis=0, keepdims=True)
            part = jnp.sum(power * dot(pair[:, head:], grad, NT), axis=0, keepdims=True)
            tops.append(top + jnp.log(total))
            deltas.append(part / total)
        stats = jnp.concatenate(tops + deltas, axis=0)
        for peer in range(stat_ref.shape[0]):
            stat_ref[peer, b] = stats
        return carry

    lax.fori_loop(0, samples, one, 0)


def forward(chips, block, scalars, src_len, tgt_len, mine, kv, mate):
    layers, _, samples, rows, _ = mine.shape
    return pl.pallas_call(
        functools.partial(forward_kernel, block),
        out_shape=kept_here(chips, samples, 2 * layers, rows, dtype=jnp.float32),
        in_specs=[SCALAR] * 3 + [FAST] * 3,
        out_specs=FAST,
        compiler_params=ROOM,
        name="forward",
    )(scalars, src_len, tgt_len, *held(mine, kv, mate))


def terms_of(grads, weights):
    terms = None
    for r in range(grads.shape[0]):
        term = dot(grads[r], weights[r], NT)
        terms = term if terms is None else terms + term
    return low(terms)


def backward_kernel(start, keys, scalars, src_len, tgt_len, mine, kv_ref, mate_ref, stat_ref, w_hbm,
                    keep_ref, give_ref, grads_ref, mate_grads_ref, *rest):
    layers, _, _ = kv_ref.shape
    rows, head = mine.shape[3:]
    half, _, _, samples, block, _ = keep_ref.shape
    scale = head ** (-0.5)
    seat, core = scalars[0], scalars[1]
    even = scalars[9] == 0
    takes = []
    if rest:
        w_ref, w_sem = rest
        part = w_ref.shape[2]
        for k in range(LEAVING):
            at = pl.ds(pl.multiple_of(scalars[4 + k] * part, part), part)
            take = pltpu.make_async_copy(w_hbm.at[:, at], w_ref.at[k], w_sem.at[k])
            take.start()
            takes.append(take)

    def one(k, carry):
        b = start + k
        stat = stat_ref[:, b]
        lse = stat[:, :layers]
        top = jnp.max(lse, axis=0)
        weight = jnp.exp(lse - top[None])
        inverse = 1.0 / jnp.sum(weight, axis=0)
        delta = jnp.sum(weight * stat[:, layers:], axis=0) * inverse
        live = live_targets(core, rows, block, head, tgt_len[b])
        key_live = key_places(seat, keys, rows) < src_len[b]
        taken = pl.ds(pl.multiple_of(b * keys, keys), keys)
        at = pl.ds(pl.multiple_of(k * keys, keys), keys)
        for r in range(layers):
            pair = jnp.concatenate([kv_ref[r, taken, :], mate_ref[r, taken, :]], axis=0)
            key, value = pair[:, :head], pair[:, head:]
            query = mine[r, 0, b]
            grad = low(jnp.where(live, wide(mine[r, 1, b]), 0.0))
            scores = jnp.where(key_live, dot(key, query, NT) * scale, masked_score)
            prob = jnp.exp(scores - top[r:r + 1, :]) * inverse[r:r + 1, :]
            slope = low(prob * (dot(value, grad, NT) - delta[r:r + 1, :]))
            prob = low(prob)
            both = (low(dot(slope, query, NN) * scale), low(dot(prob, grad, NN)))
            for side in range(2):
                columns = slice(side * head, (side + 1) * head)
                grads_ref[r, at, columns] = both[side][:keys]
                mate_grads_ref[r, at, columns] = both[side][keys:]
            for kind, out in enumerate((dot(prob, value, TN), dot(slope, key, TN) * scale)):
                out = out.reshape(half, 2, block, head)
                keep_ref[:, kind, r, k] = low(jnp.where(even, out[:, 0], out[:, 1]))
                give_ref[:, kind, r, k] = low(jnp.where(even, out[:, 1], out[:, 0]))
        return carry

    lax.fori_loop(0, samples, one, 0)
    for take in takes:
        take.wait()


def backward(chunk, block, scalars, src_len, tgt_len, mine, kv, mate, stats, weights):
    layers, _, samples, rows, head = mine.shape
    keys = kv.shape[1] // samples
    samples = samples // CHUNKS
    half = kept_here(rows // block // 2, 2, layers, samples, block, head)
    grads = kept_here(layers, samples * keys, kv.shape[2])
    outs = (half, half, grads, grads)
    scratch = []
    if chunk == 0:
        outs += (kept_here(LEAVING, layers, weights.shape[1] // 4, weights.shape[2]),)
        scratch = [pltpu.SemaphoreType.DMA((LEAVING,))]
    return pl.pallas_call(
        functools.partial(backward_kernel, chunk * samples, keys),
        out_shape=outs,
        in_specs=[SCALAR] * 3 + [FAST] * 4 + [SLOW],
        out_specs=(FAST,) * len(outs),
        scratch_shapes=scratch,
        compiler_params=ROOM,
    )(scalars, src_len, tgt_len, *held(mine, kv, mate, stats), in_hbm(weights))


def join_kernel(keys, grads_in, came, w_ref, grads, up_ref, down_ref):
    grads[...] = low(wide(grads_in[...]) + wide(came[...]))
    terms = terms_of(grads, w_ref.at[0])
    half = keys // 2
    for k in range(grads.shape[1] // keys):
        up_ref[k * half:(k + 1) * half] = terms[k * keys:k * keys + half]
        down_ref[k * half:(k + 1) * half] = terms[k * keys + half:(k + 1) * keys]


def join(keys, grads, came, weights):
    far = kept_here(grads.shape[1] // 2, weights.shape[2])
    outs = (kept_here(*grads.shape), far, far)
    return pl.pallas_call(
        functools.partial(join_kernel, keys),
        out_shape=outs,
        in_specs=[FAST] * 3,
        out_specs=(FAST,) * 3,
        compiler_params=ROOM,
    )(*held(grads, came, weights))


def near_kernel(keys, grads, w_ref, add_up, dir_up, dir_down, add_down):
    half = keys // 2
    for side, (first, second) in enumerate(((add_up, dir_up), (dir_down, add_down))):
        terms = terms_of(grads, w_ref.at[1 + side])
        for k in range(grads.shape[1] // keys):
            first[k * half:(k + 1) * half] = terms[k * keys:k * keys + half]
            second[k * half:(k + 1) * half] = terms[k * keys + half:(k + 1) * keys]


def near(keys, grads, weights):
    out = kept_here(grads.shape[1] // 2, weights.shape[2])
    return pl.pallas_call(
        functools.partial(near_kernel, keys),
        out_shape=(out,) * 4,
        in_specs=[FAST] * 2,
        out_specs=(FAST,) * 4,
        compiler_params=ROOM,
    )(*held(grads, weights))


def here_kernel(scalars, *refs):
    grads, (w_hbm, out_ref, w_ref, w_sem) = refs[:-4], refs[-4:]
    part = w_ref.shape[1]
    at = pl.ds(pl.multiple_of(scalars[7] * part, part), part)
    take = pltpu.make_async_copy(w_hbm.at[:, at], w_ref, w_sem)
    take.start()
    take.wait()
    size = grads[0].shape[1]
    for k, part in enumerate(grads):
        out_ref[k * size:(k + 1) * size] = terms_of(part, w_ref)


def here(scalars, grads, weights):
    layers, width, cols = weights.shape
    count = sum(g.shape[1] for g in grads)
    return pl.pallas_call(
        here_kernel,
        out_shape=kept_here(count, width // 4),
        in_specs=[SCALAR] + [FAST] * len(grads) + [SLOW],
        out_specs=FAST,
        scratch_shapes=[pltpu.VMEM((layers, width // 4, cols), jnp.bfloat16), pltpu.SemaphoreType.DMA],
        compiler_params=ROOM,
        name="here",
    )(scalars, *held(*grads), in_hbm(weights))


def halve_kernel(parts, run, side, *refs):
    kept, came = refs[:parts], refs[parts:2 * parts]
    keep_ref, give_ref = refs[2 * parts:]
    size = keep_ref.shape[3] // parts
    for start in range(0, keep_ref.shape[0], run):
        mine = pl.ds(2 * start + side[0] * run, run)
        other = pl.ds(2 * start + (1 - side[0]) * run, run)
        to = slice(start, start + run)
        for k in range(parts):
            at = slice(k * size, (k + 1) * size)
            keep_ref[to, :, :, at] = low(wide(kept[k][mine]) + wide(came[k][mine]))
            give_ref[to, :, :, at] = low(wide(kept[k][other]) + wide(came[k][other]))


def halve(side, kept, came, run):
    parts = len(kept)
    count, kinds, layers, samples, rows, head = kept[0].shape
    out = kept_here(count // 2, kinds, layers, samples * parts, rows, head)
    return pl.pallas_call(
        functools.partial(halve_kernel, parts, run),
        out_shape=(out, out),
        in_specs=[SCALAR] + [FAST] * (2 * parts),
        out_specs=(FAST, FAST),
        compiler_params=ROOM,
    )(side.reshape(1), *held(*kept, *came))


def deal_kernel(scalars, kept, came, *outs):
    for k, ref in enumerate(outs):
        layer = lax.rem(scalars[2] + k, len(outs))
        ref[...] = low(wide(kept[0, :, layer]) + wide(came[0, :, layer]))


def deal(scalars, kept, came):
    _, kinds, layers, samples, rows, head = kept.shape
    outs = (kept_here(kinds, samples, rows, head),) * layers
    return pl.pallas_call(
        deal_kernel, out_shape=outs, in_specs=[SCALAR, FAST, FAST], out_specs=(FAST,) * layers, compiler_params=ROOM, name="deal"
    )(scalars, *held(kept, came))


def pass_kernel(add_up, from_down, add_down, from_up, up_ref, down_ref):
    up_ref[...] = low(wide(add_up[...]) + wide(from_down[...]))
    down_ref[...] = low(wide(add_down[...]) + wide(from_up[...]))


def pass_on(add_up, from_down, add_down, from_up):
    out = kept_here(*add_up.shape)
    return pl.pallas_call(
        pass_kernel,
        out_shape=(out, out),
        in_specs=[FAST] * 4,
        out_specs=(FAST, FAST),
        compiler_params=ROOM,
    )(*held(add_up, from_down, add_down, from_up))


def gather_kernel(keys, own, *refs):
    out_ref = refs[-1]
    heads, _, part = out_ref.shape
    half = keys // 2
    for c in range(CHUNKS):
        arrived = refs[4 * c:4 * c + 4]
        for k in range(arrived[0].shape[0] // half):
            came = slice(k * half, (k + 1) * half)
            for side in range(2):
                start = (c * (arrived[0].shape[0] // half) + k) * keys + side * half
                to = slice(start, start + half)
                for h in range(heads):
                    at = slice(h * part, (h + 1) * part)
                    total = wide(own[to, at]) + wide(arrived[2 * side][came, at])
                    out_ref[h, to] = low(total + wide(arrived[2 * side + 1][came, at]))


def gather(keys, own, arrived, heads):
    count, width = own.shape
    return pl.pallas_call(
        functools.partial(gather_kernel, keys),
        out_shape=kept_here(heads, count, width // heads),
        in_specs=[FAST] * (1 + len(arrived)),
        out_specs=FAST,
        compiler_params=ROOM,
        name="gather",
    )(*held(own, *arrived))


def finish_kernel(*refs):
    out_ref = refs[-1]
    start = 0
    for ref in refs[:-1]:
        total = wide(ref[0])
        for h in range(1, ref.shape[0]):
            total = total + wide(ref[h])
        out_ref[start:start + ref.shape[1]] = low(total)
        start += ref.shape[1]


def finish(pieces):
    return pl.pallas_call(
        finish_kernel,
        out_shape=bf(sum(p.shape[1] for p in pieces), pieces[0].shape[2]),
        in_specs=[FAST] * len(pieces),
        out_specs=FAST,
        compiler_params=ROOM,
        name="finish",
    )(*held(*pieces))


def turn(count, by):
    return [(i, (i + by) % count) for i in range(count)]


def flip(count, bit):
    return [(i, i ^ bit) for i in range(count)]


def body(encoder_states, w_kv, queries, cotangent, src_len, tgt_len):
    sec = lax.axis_index("section")
    seat = lax.axis_index("seq")
    shards = lax.axis_size("seq")
    samples, src_rows, width = encoder_states.shape
    _, _, cols = w_kv.shape
    rows = queries.shape[2]
    half = rows // 2
    core = seat % 2
    places = [(sec + by) % 4 for by in (2, 1, 3, 0)]
    bits = [(seat // (1 << k)) % 2 for k in range(4)]
    scalars = jnp.stack([seat, core, sec, sec, *places, *bits]).astype(jnp.int32)

    def up(a):
        return lax.ppermute(a, "section", turn(4, 1))

    def down(a):
        return lax.ppermute(a, "section", turn(4, 3))

    def swap(a, axis):
        return lax.all_to_all(a, axis, 0, 0, tiled=True)

    block = rows // shards
    halves = []
    for source in (queries, cotangent):
        picked = source[0].reshape(samples, shards // 2, 2, block, *source.shape[3:])
        picked = lax.dynamic_index_in_dim(picked, core, 2, keepdims=False)
        picked = picked.reshape(samples, half, *source.shape[3:])
        halves.append(jnp.transpose(picked, (2, 0, 1, 3)))
    mine = swap(jnp.stack(halves, 1), "section")
    kv = project(encoder_states.reshape(samples * src_rows, width), w_kv)
    mate = lax.ppermute(kv, "seq", flip(shards, 1))
    mine, kv = lax.optimization_barrier((mine, kv))
    stats = forward(shards // 2, block, scalars, src_len, tgt_len, mine, kv, mate)
    same_core = [list(range(c, shards, 2)) for c in range(2)]
    stats = lax.all_to_all(stats, "seq", 0, 0, axis_index_groups=same_core, tiled=True)

    heads = lax.axis_size("head")
    kept, came, grads, arrived = [], [], [], []
    for c in range(CHUNKS):
        keep, give, own, other, *copied = backward(
            c, block, scalars, src_len, tgt_len, mine, kv, mate, stats, w_kv
        )
        if copied:
            (leaving,) = copied
        other = lax.ppermute(other, "seq", flip(shards, 1))
        came.append(lax.ppermute(give, "seq", flip(shards, 2)))
        kept.append(keep)
        part, far_up, far_down = join(src_rows, own, other, leaving)
        grads.append(part)
        far_up, far_down = up(far_up), down(far_down)
        add_up, dir_up, dir_down, add_down = near(src_rows, part, leaving)
        dir_up, dir_down = up(dir_up), down(dir_down)
        add_up, add_down = pass_on(add_up, far_up, add_down, far_down)
        add_up, add_down = up(add_up), down(add_down)
        arrived += [add_up, dir_down, dir_up, add_down]
    own = here(scalars, grads, w_kv)
    joined = gather(src_rows, own, arrived, heads)
    pieces = [swap(joined, "head")]
    source_grads = finish(pieces).reshape(samples, src_rows, cols)

    for bit, run in ((3, 2), (2, 1)):
        keep, give = halve(bits[bit].astype(jnp.int32), kept, came, run)
        kept, came = [keep], [lax.ppermute(give, "seq", flip(shards, 1 << bit))]
    own, to_up, to_far, to_down = deal(scalars, kept[0], came[0])
    from_down, from_up = up(to_up), down(to_down)
    from_far = lax.ppermute(to_far, "section", turn(4, 2))
    ring = jnp.stack([own, from_down, from_far, from_up])
    groups = [lax.dynamic_index_in_dim(ring, (sec + 4 - g) % 4, 0, keepdims=False) for g in range(4)]
    od = jnp.stack(groups, axis=3)
    return od[0][None], od[1][None], source_grads


def solution(mesh):
    placed = (
        P(None, "seq", None),
        P(None, None, ("section", "head")),
        P("section", None, None, None, "head"),
        P("section", None, None, None, "head"),
        P(),
        P(),
    )

    return jax.shard_map(
        body,
        mesh=mesh,
        in_specs=placed,
        out_specs=(
            P("section", None, "seq", None, "head"),
            P("section", None, "seq", None, "head"),
            P(None, "seq", ("section", "head")),
        ),
        check_vma=False,
    )
```

```python
import functools

import jax
import jax.numpy as jnp
from jax import lax
from jax.experimental import pallas as pl
from jax.experimental.pallas import tpu as pltpu
from jax.sharding import PartitionSpec as P


masked_score = -1e30
NT = (((1,), (1,)), ((), ()))
NN = (((1,), (0,)), ((), ()))
TN = (((0,), (0,)), ((), ()))
CHUNKS = 2
LEAVING = 3


def dot(a, b, dims):
    return lax.dot_general(a, b, dims, preferred_element_type=jnp.float32)


def low(a):
    return a.astype(jnp.bfloat16)


def wide(a):
    return a.astype(jnp.float32)


def bf(*shape):
    return jax.ShapeDtypeStruct(shape, jnp.bfloat16)


def kept_here(*shape, dtype=jnp.bfloat16):
    return pltpu.VMEM(shape, dtype)


def held(*arrays):
    return [pltpu.with_memory_space_constraint(a, pltpu.VMEM) for a in arrays]


def in_hbm(array):
    return pltpu.with_memory_space_constraint(array, pltpu.HBM)


ROOM = pltpu.CompilerParams(vmem_limit_bytes=16 * 1024 * 1024)
FAST = pl.BlockSpec(memory_space=pltpu.VMEM)
SLOW = pl.BlockSpec(memory_space=pl.ANY)
SCALAR = pl.BlockSpec(memory_space=pltpu.SMEM)


def project_kernel(x_ref, w_ref, out_ref):
    out_ref[pl.program_id(0)] = low(dot(x_ref[...], w_ref[0], NN))


def project(rows, w_kv):
    layers, width, cols = w_kv.shape
    count = rows.shape[0]
    return pl.pallas_call(
        project_kernel,
        out_shape=kept_here(layers, count, cols),
        grid=(layers,),
        in_specs=[
            pl.BlockSpec((count, width), lambda r: (0, 0)),
            pl.BlockSpec((1, width, cols), lambda r: (r, 0, 0)),
        ],
        out_specs=FAST,
        compiler_params=ROOM,
        name="project",
    )(in_hbm(rows), in_hbm(w_kv))


def key_places(seat, keys, targets):
    at = lax.broadcasted_iota(jnp.int32, (2 * keys, targets), 0)
    other = seat + 1 - 2 * lax.rem(seat, 2)
    return at + jnp.where(at < keys, seat * keys, other * keys - keys)


def live_targets(core, targets, block, head, limit):
    at = lax.broadcasted_iota(jnp.int32, (targets, head), 0)
    return (at // block) * (2 * block) + core * block + lax.rem(at, block) < limit


def forward_kernel(block, scalars, src_len, tgt_len, mine, kv_ref, mate_ref, stat_ref):
    seat, core = scalars[0], scalars[1]
    layers, count, _ = kv_ref.shape
    _, _, samples, rows, head = mine.shape
    keys = count // samples
    scale = head ** (-0.5)

    def one(b, carry):
        live = live_targets(core, rows, block, head, tgt_len[b])
        key_live = key_places(seat, keys, rows) < src_len[b]
        at = pl.ds(pl.multiple_of(b * keys, keys), keys)
        tops, deltas = [], []
        for r in range(layers):
            query = mine[r, 0, b]
            grad = low(jnp.where(live, wide(mine[r, 1, b]), 0.0))
            pair = jnp.concatenate([kv_ref[r, at, :], mate_ref[r, at, :]], axis=0)
            scores = jnp.where(key_live, dot(pair[:, :head], query, NT) * scale, masked_score)
            top = jnp.max(scores, axis=0, keepdims=True)
            power = jnp.exp(scores - top)
            total = jnp.sum(power, axis=0, keepdims=True)
            part = jnp.sum(power * dot(pair[:, head:], grad, NT), axis=0, keepdims=True)
            tops.append(top + jnp.log(total))
            deltas.append(part / total)
        stats = jnp.concatenate(tops + deltas, axis=0)
        for peer in range(stat_ref.shape[0]):
            stat_ref[peer, b] = stats
        return carry

    lax.fori_loop(0, samples, one, 0)


def forward(chips, block, scalars, src_len, tgt_len, mine, kv, mate):
    layers, _, samples, rows, _ = mine.shape
    return pl.pallas_call(
        functools.partial(forward_kernel, block),
        out_shape=kept_here(chips, samples, 2 * layers, rows, dtype=jnp.float32),
        in_specs=[SCALAR] * 3 + [FAST] * 3,
        out_specs=FAST,
        compiler_params=ROOM,
        name="forward",
    )(scalars, src_len, tgt_len, *held(mine, kv, mate))


def terms_of(grads, weights):
    terms = None
    for r in range(grads.shape[0]):
        term = dot(grads[r], weights[r], NT)
        terms = term if terms is None else terms + term
    return low(terms)


def backward_kernel(start, keys, scalars, src_len, tgt_len, mine, kv_ref, mate_ref, stat_ref, w_hbm,
                    keep_ref, give_ref, grads_ref, mate_grads_ref, *rest):
    layers, _, _ = kv_ref.shape
    rows, head = mine.shape[3:]
    half, _, _, samples, block, _ = keep_ref.shape
    scale = head ** (-0.5)
    seat, core = scalars[0], scalars[1]
    low_side = scalars[11] == 0
    takes = []
    if rest:
        w_ref, w_sem = rest
        part = w_ref.shape[2]
        for k in range(LEAVING):
            at = pl.ds(pl.multiple_of(scalars[4 + k] * part, part), part)
            take = pltpu.make_async_copy(w_hbm.at[:, at], w_ref.at[k], w_sem.at[k])
            take.start()
            takes.append(take)

    def one(k, carry):
        b = start + k
        stat = stat_ref[:, b]
        lse = stat[:, :layers]
        top = jnp.max(lse, axis=0)
        weight = jnp.exp(lse - top[None])
        inverse = 1.0 / jnp.sum(weight, axis=0)
        delta = jnp.sum(weight * stat[:, layers:], axis=0) * inverse
        live = live_targets(core, rows, block, head, tgt_len[b])
        key_live = key_places(seat, keys, rows) < src_len[b]
        taken = pl.ds(pl.multiple_of(b * keys, keys), keys)
        at = pl.ds(pl.multiple_of(k * keys, keys), keys)
        for r in range(layers):
            pair = jnp.concatenate([kv_ref[r, taken, :], mate_ref[r, taken, :]], axis=0)
            key, value = pair[:, :head], pair[:, head:]
            query = mine[r, 0, b]
            grad = low(jnp.where(live, wide(mine[r, 1, b]), 0.0))
            scores = jnp.where(key_live, dot(key, query, NT) * scale, masked_score)
            prob = jnp.exp(scores - top[r:r + 1, :]) * inverse[r:r + 1, :]
            slope = low(prob * (dot(value, grad, NT) - delta[r:r + 1, :]))
            prob = low(prob)
            both = (low(dot(slope, query, NN) * scale), low(dot(prob, grad, NN)))
            for side in range(2):
                columns = slice(side * head, (side + 1) * head)
                grads_ref[r, at, columns] = both[side][:keys]
                mate_grads_ref[r, at, columns] = both[side][keys:]
            for kind, out in enumerate((dot(prob, value, TN), dot(slope, key, TN) * scale)):
                out = out.reshape(2, half, block, head)
                keep_ref[:, kind, r, k] = low(jnp.where(low_side, out[0], out[1]))
                give_ref[:, kind, r, k] = low(jnp.where(low_side, out[1], out[0]))
        return carry

    lax.fori_loop(0, samples, one, 0)
    for take in takes:
        take.wait()


def backward(chunk, block, scalars, src_len, tgt_len, mine, kv, mate, stats, weights):
    layers, _, samples, rows, head = mine.shape
    keys = kv.shape[1] // samples
    samples = samples // CHUNKS
    half = kept_here(rows // block // 2, 2, layers, samples, block, head)
    grads = kept_here(layers, samples * keys, kv.shape[2])
    outs = (half, half, grads, grads)
    scratch = []
    if chunk == 0:
        outs += (kept_here(LEAVING, layers, weights.shape[1] // 4, weights.shape[2]),)
        scratch = [pltpu.SemaphoreType.DMA((LEAVING,))]
    return pl.pallas_call(
        functools.partial(backward_kernel, chunk * samples, keys),
        out_shape=outs,
        in_specs=[SCALAR] * 3 + [FAST] * 4 + [SLOW],
        out_specs=(FAST,) * len(outs),
        scratch_shapes=scratch,
        compiler_params=ROOM,
    )(scalars, src_len, tgt_len, *held(mine, kv, mate, stats), in_hbm(weights))


def join_kernel(keys, grads_in, came, w_ref, grads, up_ref, down_ref):
    grads[...] = low(wide(grads_in[...]) + wide(came[...]))
    terms = terms_of(grads, w_ref.at[0])
    half = keys // 2
    for k in range(grads.shape[1] // keys):
        up_ref[k * half:(k + 1) * half] = terms[k * keys:k * keys + half]
        down_ref[k * half:(k + 1) * half] = terms[k * keys + half:(k + 1) * keys]


def join(keys, grads, came, weights):
    far = kept_here(grads.shape[1] // 2, weights.shape[2])
    outs = (kept_here(*grads.shape), far, far)
    return pl.pallas_call(
        functools.partial(join_kernel, keys),
        out_shape=outs,
        in_specs=[FAST] * 3,
        out_specs=(FAST,) * 3,
        compiler_params=ROOM,
    )(*held(grads, came, weights))


def near_kernel(keys, grads, w_ref, add_up, dir_up, dir_down, add_down):
    half = keys // 2
    for side, (first, second) in enumerate(((add_up, dir_up), (dir_down, add_down))):
        terms = terms_of(grads, w_ref.at[1 + side])
        for k in range(grads.shape[1] // keys):
            first[k * half:(k + 1) * half] = terms[k * keys:k * keys + half]
            second[k * half:(k + 1) * half] = terms[k * keys + half:(k + 1) * keys]


def near(keys, grads, weights):
    out = kept_here(grads.shape[1] // 2, weights.shape[2])
    return pl.pallas_call(
        functools.partial(near_kernel, keys),
        out_shape=(out,) * 4,
        in_specs=[FAST] * 2,
        out_specs=(FAST,) * 4,
        compiler_params=ROOM,
    )(*held(grads, weights))


def here_kernel(scalars, grads, w_hbm, out_ref, w_ref, w_sem):
    part = w_ref.shape[1]
    at = pl.ds(pl.multiple_of(scalars[7] * part, part), part)
    take = pltpu.make_async_copy(w_hbm.at[:, at], w_ref, w_sem)
    take.start()
    take.wait()
    out_ref[...] = terms_of(grads, w_ref)


def here(scalars, grads, weights):
    layers, width, cols = weights.shape
    return pl.pallas_call(
        here_kernel,
        out_shape=kept_here(grads.shape[1], width // 4),
        in_specs=[SCALAR, FAST, SLOW],
        out_specs=FAST,
        scratch_shapes=[pltpu.VMEM((layers, width // 4, cols), jnp.bfloat16), pltpu.SemaphoreType.DMA],
        compiler_params=ROOM,
    )(scalars, *held(grads), in_hbm(weights))


def halve_kernel(parts, run, side, *refs):
    kept, came = refs[:parts], refs[parts:2 * parts]
    keep_ref, give_ref = refs[2 * parts:]
    size = keep_ref.shape[3] // parts
    for start in range(0, keep_ref.shape[0], run):
        mine = pl.ds(2 * start + side[0] * run, run)
        other = pl.ds(2 * start + (1 - side[0]) * run, run)
        to = slice(start, start + run)
        for k in range(parts):
            at = slice(k * size, (k + 1) * size)
            keep_ref[to, :, :, at] = low(wide(kept[k][mine]) + wide(came[k][mine]))
            give_ref[to, :, :, at] = low(wide(kept[k][other]) + wide(came[k][other]))


def halve(side, kept, came, run):
    parts = len(kept)
    count, kinds, layers, samples, rows, head = kept[0].shape
    out = kept_here(count // 2, kinds, layers, samples * parts, rows, head)
    return pl.pallas_call(
        functools.partial(halve_kernel, parts, run),
        out_shape=(out, out),
        in_specs=[SCALAR] + [FAST] * (2 * parts),
        out_specs=(FAST, FAST),
        compiler_params=ROOM,
    )(side.reshape(1), *held(*kept, *came))


def deal_kernel(scalars, kept, came, *outs):
    for k, ref in enumerate(outs):
        layer = lax.rem(scalars[2] + k, len(outs))
        ref[...] = low(wide(kept[0, :, layer]) + wide(came[0, :, layer]))


def deal(scalars, kept, came):
    _, kinds, layers, samples, rows, head = kept.shape
    outs = (kept_here(kinds, samples, rows, head),) * layers
    return pl.pallas_call(
        deal_kernel, out_shape=outs, in_specs=[SCALAR, FAST, FAST], out_specs=(FAST,) * layers, compiler_params=ROOM, name="deal"
    )(scalars, *held(kept, came))


def pass_kernel(add_up, from_down, add_down, from_up, up_ref, down_ref):
    up_ref[...] = low(wide(add_up[...]) + wide(from_down[...]))
    down_ref[...] = low(wide(add_down[...]) + wide(from_up[...]))


def pass_on(add_up, from_down, add_down, from_up):
    out = kept_here(*add_up.shape)
    return pl.pallas_call(
        pass_kernel,
        out_shape=(out, out),
        in_specs=[FAST] * 4,
        out_specs=(FAST, FAST),
        compiler_params=ROOM,
    )(*held(add_up, from_down, add_down, from_up))


def gather_kernel(keys, own, *refs):
    arrived, out_ref = refs[:-1], refs[-1]
    heads, count, part = out_ref.shape
    half = keys // 2
    for k in range(count // keys):
        came = slice(k * half, (k + 1) * half)
        for side in range(2):
            to = slice(k * keys + side * half, k * keys + (side + 1) * half)
            for h in range(heads):
                at = slice(h * part, (h + 1) * part)
                total = wide(own[to, at]) + wide(arrived[2 * side][came, at])
                out_ref[h, to] = low(total + wide(arrived[2 * side + 1][came, at]))


def gather(keys, own, arrived, heads):
    count, width = own.shape
    return pl.pallas_call(
        functools.partial(gather_kernel, keys),
        out_shape=kept_here(heads, count, width // heads),
        in_specs=[FAST] * (1 + len(arrived)),
        out_specs=FAST,
        compiler_params=ROOM,
    )(*held(own, *arrived))


def finish_kernel(*refs):
    out_ref = refs[-1]
    start = 0
    for ref in refs[:-1]:
        total = wide(ref[0])
        for h in range(1, ref.shape[0]):
            total = total + wide(ref[h])
        out_ref[start:start + ref.shape[1]] = low(total)
        start += ref.shape[1]


def finish(pieces):
    return pl.pallas_call(
        finish_kernel,
        out_shape=bf(sum(p.shape[1] for p in pieces), pieces[0].shape[2]),
        in_specs=[FAST] * len(pieces),
        out_specs=FAST,
        compiler_params=ROOM,
        name="finish",
    )(*held(*pieces))


def turn(count, by):
    return [(i, (i + by) % count) for i in range(count)]


def flip(count, bit):
    return [(i, i ^ bit) for i in range(count)]


def body(encoder_states, w_kv, queries, cotangent, src_len, tgt_len):
    sec = lax.axis_index("section")
    seat = lax.axis_index("seq")
    shards = lax.axis_size("seq")
    samples, src_rows, width = encoder_states.shape
    _, _, cols = w_kv.shape
    rows = queries.shape[2]
    half = rows // 2
    core = seat % 2
    places = [(sec + by) % 4 for by in (2, 1, 3, 0)]
    bits = [(seat // (1 << k)) % 2 for k in range(4)]
    scalars = jnp.stack([seat, core, sec, sec, *places, *bits]).astype(jnp.int32)

    def up(a):
        return lax.ppermute(a, "section", turn(4, 1))

    def down(a):
        return lax.ppermute(a, "section", turn(4, 3))

    def swap(a, axis):
        return lax.all_to_all(a, axis, 0, 0, tiled=True)

    block = rows // shards
    halves = []
    for source in (queries, cotangent):
        picked = source[0].reshape(samples, shards // 2, 2, block, *source.shape[3:])
        picked = lax.dynamic_index_in_dim(picked, core, 2, keepdims=False)
        picked = picked.reshape(samples, half, *source.shape[3:])
        halves.append(jnp.transpose(picked, (2, 0, 1, 3)))
    mine = swap(jnp.stack(halves, 1), "section")
    kv = project(encoder_states.reshape(samples * src_rows, width), w_kv)
    mate = lax.ppermute(kv, "seq", flip(shards, 1))
    mine, kv = lax.optimization_barrier((mine, kv))
    stats = forward(shards // 2, block, scalars, src_len, tgt_len, mine, kv, mate)
    same_core = [list(range(c, shards, 2)) for c in range(2)]
    stats = lax.all_to_all(stats, "seq", 0, 0, axis_index_groups=same_core, tiled=True)

    heads = lax.axis_size("head")
    kept, came, pieces = [], [], []
    for c in range(CHUNKS):
        keep, give, own, other, *copied = backward(
            c, block, scalars, src_len, tgt_len, mine, kv, mate, stats, w_kv
        )
        if copied:
            (leaving,) = copied
        other = lax.ppermute(other, "seq", flip(shards, 1))
        came.append(lax.ppermute(give, "seq", flip(shards, 8)))
        kept.append(keep)
        part, far_up, far_down = join(src_rows, own, other, leaving)
        far_up, far_down = up(far_up), down(far_down)
        add_up, dir_up, dir_down, add_down = near(src_rows, part, leaving)
        dir_up, dir_down = up(dir_up), down(dir_down)
        add_up, add_down = pass_on(add_up, far_up, add_down, far_down)
        add_up, add_down = up(add_up), down(add_down)
        own = here(scalars, part, w_kv)
        joined = gather(src_rows, own, [add_up, dir_down, dir_up, add_down], heads)
        pieces.append(swap(joined, "head"))
    source_grads = finish(pieces).reshape(samples, src_rows, cols)

    for bit, run in ((1, 1), (2, 1)):
        keep, give = halve(bits[bit].astype(jnp.int32), kept, came, run)
        kept, came = [keep], [lax.ppermute(give, "seq", flip(shards, 1 << bit))]
    own, to_up, to_far, to_down = deal(scalars, kept[0], came[0])
    from_down, from_up = up(to_up), down(to_down)
    from_far = lax.ppermute(to_far, "section", turn(4, 2))
    ring = jnp.stack([own, from_down, from_far, from_up])
    groups = [lax.dynamic_index_in_dim(ring, (sec + 4 - g) % 4, 0, keepdims=False) for g in range(4)]
    od = jnp.stack(groups, axis=3)
    return od[0][None], od[1][None], source_grads


def solution(mesh):
    placed = (
        P(None, "seq", None),
        P(None, None, ("section", "head")),
        P("section", None, None, None, "head"),
        P("section", None, None, None, "head"),
        P(),
        P(),
    )

    return jax.shard_map(
        body,
        mesh=mesh,
        in_specs=placed,
        out_specs=(
            P("section", None, "seq", None, "head"),
            P("section", None, "seq", None, "head"),
            P(None, "seq", ("section", "head")),
        ),
        check_vma=False,
    )
```

```python
import functools

import jax
import jax.numpy as jnp
from jax import lax
from jax.experimental import pallas as pl
from jax.experimental.pallas import tpu as pltpu
from jax.sharding import PartitionSpec as P


masked_score = -1e30
NT = (((1,), (1,)), ((), ()))
NN = (((1,), (0,)), ((), ()))
TN = (((0,), (0,)), ((), ()))
CHUNKS = 2
GROUPED = (1, 3)
LEAVING = 3


def dot(a, b, dims):
    return lax.dot_general(a, b, dims, preferred_element_type=jnp.float32)


def low(a):
    return a.astype(jnp.bfloat16)


def wide(a):
    return a.astype(jnp.float32)


def bf(*shape):
    return jax.ShapeDtypeStruct(shape, jnp.bfloat16)


def kept_here(*shape, dtype=jnp.bfloat16):
    return pltpu.VMEM(shape, dtype)


def held(*arrays):
    return [pltpu.with_memory_space_constraint(a, pltpu.VMEM) for a in arrays]


def in_hbm(array):
    return pltpu.with_memory_space_constraint(array, pltpu.HBM)


ROOM = pltpu.CompilerParams(vmem_limit_bytes=16 * 1024 * 1024)
FAST = pl.BlockSpec(memory_space=pltpu.VMEM)
SLOW = pl.BlockSpec(memory_space=pl.ANY)
SCALAR = pl.BlockSpec(memory_space=pltpu.SMEM)


def project_kernel(x_ref, w_ref, out_ref):
    out_ref[pl.program_id(0)] = low(dot(x_ref[...], w_ref[0], NN))


def project(rows, w_kv):
    layers, width, cols = w_kv.shape
    count = rows.shape[0]
    return pl.pallas_call(
        project_kernel,
        out_shape=kept_here(layers, count, cols),
        grid=(layers,),
        in_specs=[
            pl.BlockSpec((count, width), lambda r: (0, 0)),
            pl.BlockSpec((1, width, cols), lambda r: (r, 0, 0)),
        ],
        out_specs=FAST,
        compiler_params=ROOM,
        name="project",
    )(in_hbm(rows), in_hbm(w_kv))


def key_places(seat, keys, targets):
    at = lax.broadcasted_iota(jnp.int32, (2 * keys, targets), 0)
    other = seat + 1 - 2 * lax.rem(seat, 2)
    return at + jnp.where(at < keys, seat * keys, other * keys - keys)


def live_targets(core, targets, block, head, limit):
    at = lax.broadcasted_iota(jnp.int32, (targets, head), 0)
    return (at // block) * (2 * block) + core * block + lax.rem(at, block) < limit


def forward_kernel(block, scalars, src_len, tgt_len, mine, kv_ref, mate_ref, stat_ref):
    seat, core = scalars[0], scalars[1]
    layers, count, _ = kv_ref.shape
    _, _, samples, rows, head = mine.shape
    keys = count // samples
    scale = head ** (-0.5)

    def one(b, carry):
        live = live_targets(core, rows, block, head, tgt_len[b])
        key_live = key_places(seat, keys, rows) < src_len[b]
        at = pl.ds(pl.multiple_of(b * keys, keys), keys)
        tops, deltas = [], []
        for r in range(layers):
            query = mine[r, 0, b]
            grad = low(jnp.where(live, wide(mine[r, 1, b]), 0.0))
            pair = jnp.concatenate([kv_ref[r, at, :], mate_ref[r, at, :]], axis=0)
            scores = jnp.where(key_live, dot(pair[:, :head], query, NT) * scale, masked_score)
            top = jnp.max(scores, axis=0, keepdims=True)
            power = jnp.exp(scores - top)
            total = jnp.sum(power, axis=0, keepdims=True)
            part = jnp.sum(power * dot(pair[:, head:], grad, NT), axis=0, keepdims=True)
            tops.append(top + jnp.log(total))
            deltas.append(part / total)
        stats = jnp.concatenate(tops + deltas, axis=0)
        for peer in range(stat_ref.shape[0]):
            stat_ref[peer, b] = stats
        return carry

    lax.fori_loop(0, samples, one, 0)


def forward(chips, block, scalars, src_len, tgt_len, mine, kv, mate):
    layers, _, samples, rows, _ = mine.shape
    return pl.pallas_call(
        functools.partial(forward_kernel, block),
        out_shape=kept_here(chips, samples, 2 * layers, rows, dtype=jnp.float32),
        in_specs=[SCALAR] * 3 + [FAST] * 3,
        out_specs=FAST,
        compiler_params=ROOM,
        name="forward",
    )(scalars, src_len, tgt_len, *held(mine, kv, mate))


def terms_of(grads, weights):
    terms = None
    for r in range(grads.shape[0]):
        term = dot(grads[r], weights[r], NT)
        terms = term if terms is None else terms + term
    return low(terms)


def backward_kernel(start, keys, scalars, src_len, tgt_len, mine, kv_ref, mate_ref, stat_ref, w_hbm,
                    keep_ref, give_ref, grads_ref, mate_grads_ref, *rest):
    layers, _, _ = kv_ref.shape
    rows, head = mine.shape[3:]
    half, _, _, samples, block, _ = keep_ref.shape
    scale = head ** (-0.5)
    seat, core = scalars[0], scalars[1]
    even = scalars[9] == 0
    takes = []
    if rest:
        w_ref, w_sem = rest
        part = w_ref.shape[2]
        for k in range(LEAVING):
            at = pl.ds(pl.multiple_of(scalars[4 + k] * part, part), part)
            take = pltpu.make_async_copy(w_hbm.at[:, at], w_ref.at[k], w_sem.at[k])
            take.start()
            takes.append(take)

    def one(k, carry):
        b = start + k
        stat = stat_ref[:, b]
        lse = stat[:, :layers]
        top = jnp.max(lse, axis=0)
        weight = jnp.exp(lse - top[None])
        inverse = 1.0 / jnp.sum(weight, axis=0)
        delta = jnp.sum(weight * stat[:, layers:], axis=0) * inverse
        live = live_targets(core, rows, block, head, tgt_len[b])
        key_live = key_places(seat, keys, rows) < src_len[b]
        taken = pl.ds(pl.multiple_of(b * keys, keys), keys)
        at = pl.ds(pl.multiple_of(k * keys, keys), keys)
        for r in range(layers):
            pair = jnp.concatenate([kv_ref[r, taken, :], mate_ref[r, taken, :]], axis=0)
            key, value = pair[:, :head], pair[:, head:]
            query = mine[r, 0, b]
            grad = low(jnp.where(live, wide(mine[r, 1, b]), 0.0))
            scores = jnp.where(key_live, dot(key, query, NT) * scale, masked_score)
            prob = jnp.exp(scores - top[r:r + 1, :]) * inverse[r:r + 1, :]
            slope = low(prob * (dot(value, grad, NT) - delta[r:r + 1, :]))
            prob = low(prob)
            both = (low(dot(slope, query, NN) * scale), low(dot(prob, grad, NN)))
            for side in range(2):
                columns = slice(side * head, (side + 1) * head)
                grads_ref[r, at, columns] = both[side][:keys]
                mate_grads_ref[r, at, columns] = both[side][keys:]
            for kind, out in enumerate((dot(prob, value, TN), dot(slope, key, TN) * scale)):
                out = out.reshape(half, 2, block, head)
                keep_ref[:, kind, r, k] = low(jnp.where(even, out[:, 0], out[:, 1]))
                give_ref[:, kind, r, k] = low(jnp.where(even, out[:, 1], out[:, 0]))
        return carry

    lax.fori_loop(0, samples, one, 0)
    for take in takes:
        take.wait()


def backward(chunk, block, scalars, src_len, tgt_len, mine, kv, mate, stats, weights):
    layers, _, samples, rows, head = mine.shape
    keys = kv.shape[1] // samples
    samples = samples // CHUNKS
    half = kept_here(rows // block // 2, 2, layers, samples, block, head)
    grads = kept_here(layers, samples * keys, kv.shape[2])
    outs = (half, half, grads, grads)
    scratch = []
    if chunk == 0:
        outs += (kept_here(LEAVING, layers, weights.shape[1] // 4, weights.shape[2]),)
        scratch = [pltpu.SemaphoreType.DMA((LEAVING,))]
    return pl.pallas_call(
        functools.partial(backward_kernel, chunk * samples, keys),
        out_shape=outs,
        in_specs=[SCALAR] * 3 + [FAST] * 4 + [SLOW],
        out_specs=(FAST,) * len(outs),
        scratch_shapes=scratch,
        compiler_params=ROOM,
    )(scalars, src_len, tgt_len, *held(mine, kv, mate, stats), in_hbm(weights))


def join_kernel(keys, grads_in, came, w_ref, grads, up_ref, down_ref):
    grads[...] = low(wide(grads_in[...]) + wide(came[...]))
    terms = terms_of(grads, w_ref.at[0])
    half = keys // 2
    for k in range(grads.shape[1] // keys):
        up_ref[k * half:(k + 1) * half] = terms[k * keys:k * keys + half]
        down_ref[k * half:(k + 1) * half] = terms[k * keys + half:(k + 1) * keys]


def join(keys, grads, came, weights):
    far = kept_here(grads.shape[1] // 2, weights.shape[2])
    outs = (kept_here(*grads.shape), far, far)
    return pl.pallas_call(
        functools.partial(join_kernel, keys),
        out_shape=outs,
        in_specs=[FAST] * 3,
        out_specs=(FAST,) * 3,
        compiler_params=ROOM,
    )(*held(grads, came, weights))


def near_kernel(*refs):
    grads, w_ref, outs = refs[:CHUNKS], refs[CHUNKS], refs[CHUNKS + 1:]
    groups = len(outs) // 2
    for side in range(2):
        done = 0
        terms = [terms_of(g, w_ref.at[1 + side]) for g in grads]
        size = terms[0].shape[0]
        for k in range(groups):
            ref = outs[side * groups + k]
            filled = 0
            while filled < ref.shape[0]:
                chunk, at = divmod(done + filled, size)
                count = min(ref.shape[0] - filled, size - at)
                ref[filled:filled + count] = terms[chunk][at:at + count]
                filled += count
            done += filled


def near(grads, weights, keys):
    outs = tuple(kept_here(g * keys, weights.shape[2]) for g in GROUPED) * 2
    return pl.pallas_call(
        near_kernel,
        out_shape=outs,
        in_specs=[FAST] * (len(grads) + 1),
        out_specs=(FAST,) * len(outs),
        compiler_params=ROOM,
        name="near",
    )(*held(*grads, weights))


def here_kernel(scalars, *refs):
    grads, (w_hbm, out_ref, w_ref, w_sem) = refs[:-4], refs[-4:]
    part = w_ref.shape[1]
    at = pl.ds(pl.multiple_of(scalars[7] * part, part), part)
    take = pltpu.make_async_copy(w_hbm.at[:, at], w_ref, w_sem)
    take.start()
    take.wait()
    size = grads[0].shape[1]
    for k, part in enumerate(grads):
        out_ref[k * size:(k + 1) * size] = terms_of(part, w_ref)


def here(scalars, grads, weights):
    layers, width, cols = weights.shape
    count = sum(g.shape[1] for g in grads)
    return pl.pallas_call(
        here_kernel,
        out_shape=kept_here(count, width // 4),
        in_specs=[SCALAR] + [FAST] * len(grads) + [SLOW],
        out_specs=FAST,
        scratch_shapes=[pltpu.VMEM((layers, width // 4, cols), jnp.bfloat16), pltpu.SemaphoreType.DMA],
        compiler_params=ROOM,
        name="here",
    )(scalars, *held(*grads), in_hbm(weights))


def halve_kernel(parts, run, side, *refs):
    kept, came = refs[:parts], refs[parts:2 * parts]
    keep_ref, give_ref = refs[2 * parts:]
    size = keep_ref.shape[3] // parts
    for start in range(0, keep_ref.shape[0], run):
        mine = pl.ds(2 * start + side[0] * run, run)
        other = pl.ds(2 * start + (1 - side[0]) * run, run)
        to = slice(start, start + run)
        for k in range(parts):
            at = slice(k * size, (k + 1) * size)
            keep_ref[to, :, :, at] = low(wide(kept[k][mine]) + wide(came[k][mine]))
            give_ref[to, :, :, at] = low(wide(kept[k][other]) + wide(came[k][other]))


def halve(side, kept, came, run):
    parts = len(kept)
    count, kinds, layers, samples, rows, head = kept[0].shape
    out = kept_here(count // 2, kinds, layers, samples * parts, rows, head)
    return pl.pallas_call(
        functools.partial(halve_kernel, parts, run),
        out_shape=(out, out),
        in_specs=[SCALAR] + [FAST] * (2 * parts),
        out_specs=(FAST, FAST),
        compiler_params=ROOM,
    )(side.reshape(1), *held(*kept, *came))


def deal_kernel(scalars, kept, came, *outs):
    for k, ref in enumerate(outs):
        layer = lax.rem(scalars[2] + k, len(outs))
        ref[...] = low(wide(kept[0, :, layer]) + wide(came[0, :, layer]))


def deal(scalars, kept, came):
    _, kinds, layers, samples, rows, head = kept.shape
    outs = (kept_here(kinds, samples, rows, head),) * layers
    return pl.pallas_call(
        deal_kernel, out_shape=outs, in_specs=[SCALAR, FAST, FAST], out_specs=(FAST,) * layers, compiler_params=ROOM, name="deal"
    )(scalars, *held(kept, came))


def pass_kernel(keys, start, up_in, down_in, *refs):
    ups, downs = refs[:(len(refs) - 2) // 2], refs[(len(refs) - 2) // 2:-2]
    up_ref, down_ref = refs[-2:]
    half = keys // 2
    per = ups[0].shape[0] // half
    first = start // per
    for k in range(up_in.shape[0] // keys):
        chunk, place = divmod(start + k, per)
        came = slice(place * half, (place + 1) * half)
        top, bottom = slice(k * keys, k * keys + half), slice(k * keys + half, (k + 1) * keys)
        up_ref[top] = low(wide(up_in[top]) + wide(ups[chunk - first][came]))
        down_ref[bottom] = low(wide(down_in[bottom]) + wide(downs[chunk - first][came]))
        up_ref[bottom] = up_in[bottom]
        down_ref[top] = down_in[top]


def pass_on(keys, start, up_in, down_in, ups, downs):
    per = ups[0].shape[0] // (keys // 2)
    last = (start + up_in.shape[0] // keys - 1) // per
    ups, downs = ups[start // per:last + 1], downs[start // per:last + 1]
    out = kept_here(*up_in.shape)
    return pl.pallas_call(
        functools.partial(pass_kernel, keys, start),
        out_shape=(out, out),
        in_specs=[FAST] * (2 + 2 * len(ups)),
        out_specs=(FAST, FAST),
        compiler_params=ROOM,
    )(*held(up_in, down_in, *ups, *downs))


def gather_kernel(start, own, from_down, from_up, out_ref):
    heads, count, part = out_ref.shape
    for h in range(heads):
        at = slice(h * part, (h + 1) * part)
        out_ref[h] = low(wide(own[start:start + count, at]) + wide(from_down[:, at]) + wide(from_up[:, at]))


def gather(start, own, from_down, from_up, heads):
    count, width = from_down.shape
    return pl.pallas_call(
        functools.partial(gather_kernel, start),
        out_shape=kept_here(heads, count, width // heads),
        in_specs=[FAST] * 3,
        out_specs=FAST,
        compiler_params=ROOM,
    )(*held(own, from_down, from_up))


def finish_kernel(*refs):
    out_ref = refs[-1]
    start = 0
    for ref in refs[:-1]:
        total = wide(ref[0])
        for h in range(1, ref.shape[0]):
            total = total + wide(ref[h])
        out_ref[start:start + ref.shape[1]] = low(total)
        start += ref.shape[1]


def finish(pieces):
    return pl.pallas_call(
        finish_kernel,
        out_shape=bf(sum(p.shape[1] for p in pieces), pieces[0].shape[2]),
        in_specs=[FAST] * len(pieces),
        out_specs=FAST,
        compiler_params=ROOM,
        name="finish",
    )(*held(*pieces))


def turn(count, by):
    return [(i, (i + by) % count) for i in range(count)]


def flip(count, bit):
    return [(i, i ^ bit) for i in range(count)]


def body(encoder_states, w_kv, queries, cotangent, src_len, tgt_len):
    sec = lax.axis_index("section")
    seat = lax.axis_index("seq")
    shards = lax.axis_size("seq")
    samples, src_rows, width = encoder_states.shape
    _, _, cols = w_kv.shape
    rows = queries.shape[2]
    half = rows // 2
    core = seat % 2
    places = [(sec + by) % 4 for by in (2, 1, 3, 0)]
    bits = [(seat // (1 << k)) % 2 for k in range(4)]
    scalars = jnp.stack([seat, core, sec, sec, *places, *bits]).astype(jnp.int32)

    def up(a):
        return lax.ppermute(a, "section", turn(4, 1))

    def down(a):
        return lax.ppermute(a, "section", turn(4, 3))

    def swap(a, axis):
        return lax.all_to_all(a, axis, 0, 0, tiled=True)

    block = rows // shards
    halves = []
    for source in (queries, cotangent):
        picked = source[0].reshape(samples, shards // 2, 2, block, *source.shape[3:])
        picked = lax.dynamic_index_in_dim(picked, core, 2, keepdims=False)
        picked = picked.reshape(samples, half, *source.shape[3:])
        halves.append(jnp.transpose(picked, (2, 0, 1, 3)))
    mine = swap(jnp.stack(halves, 1), "section")
    kv = project(encoder_states.reshape(samples * src_rows, width), w_kv)
    mate = lax.ppermute(kv, "seq", flip(shards, 1))
    mine, kv = lax.optimization_barrier((mine, kv))
    stats = forward(shards // 2, block, scalars, src_len, tgt_len, mine, kv, mate)
    same_core = [list(range(c, shards, 2)) for c in range(2)]
    stats = lax.all_to_all(stats, "seq", 0, 0, axis_index_groups=same_core, tiled=True)

    heads = lax.axis_size("head")
    kept, came, parts, grads, ups, downs = [], [], [], [], [], []
    weights = w_kv
    for c in range(CHUNKS):
        keep, give, own, other, *copied = backward(
            c, block, scalars, src_len, tgt_len, mine, kv, mate, stats, w_kv
        )
        weights = copied[0] if copied else weights
        parts.append((own, lax.ppermute(other, "seq", flip(shards, 1))))
        came.append(lax.ppermute(give, "seq", flip(shards, 2)))
        kept.append(keep)
    for c in range(CHUNKS):
        part, far_up, far_down = join(src_rows, *parts[c], weights)
        ups.append(up(far_up))
        downs.append(down(far_down))
        grads.append(part)
    sides = near(grads, weights, src_rows)
    own = here(scalars, grads, w_kv)
    pieces = []
    start = 0
    for c, group in enumerate(GROUPED):
        to_up, to_down = pass_on(src_rows, start, sides[c], sides[len(GROUPED) + c], ups, downs)
        to_up, to_down = up(to_up), down(to_down)
        joined = gather(start * src_rows, own, to_up, to_down, heads)
        pieces.append(swap(joined, "head"))
        start += group
    source_grads = finish(pieces).reshape(samples, src_rows, cols)

    for bit, run in ((3, 2), (2, 1)):
        keep, give = halve(bits[bit].astype(jnp.int32), kept, came, run)
        kept, came = [keep], [lax.ppermute(give, "seq", flip(shards, 1 << bit))]
    own, to_up, to_far, to_down = deal(scalars, kept[0], came[0])
    from_down, from_up = up(to_up), down(to_down)
    from_far = lax.ppermute(to_far, "section", turn(4, 2))
    ring = jnp.stack([own, from_down, from_far, from_up])
    groups = [lax.dynamic_index_in_dim(ring, (sec + 4 - g) % 4, 0, keepdims=False) for g in range(4)]
    od = jnp.stack(groups, axis=3)
    return od[0][None], od[1][None], source_grads


def solution(mesh):
    placed = (
        P(None, "seq", None),
        P(None, None, ("section", "head")),
        P("section", None, None, None, "head"),
        P("section", None, None, None, "head"),
        P(),
        P(),
    )

    return jax.shard_map(
        body,
        mesh=mesh,
        in_specs=placed,
        out_specs=(
            P("section", None, "seq", None, "head"),
            P("section", None, "seq", None, "head"),
            P(None, "seq", ("section", "head")),
        ),
        check_vma=False,
    )
```
